256 devices in a mesh: dp: 64 (over z, y, core), mp: 4 (over x).
Axes of the slice: x: 4, y: 4, z: 8, core: 2. Of those that a mesh axis runs over, the one named last changes fastest.
Arguments:
- tokens: bfloat16 [49152, 768], P(('dp', 'mp')), may hold values from -6 to 6
- obs_mask: int32 [768, 64], P(('dp', 'mp')), may hold values 0 or 1
- norm_gains: float32 [5, 768], replicated, may hold values from 0.1 to 1.9
- attn_in: bfloat16 [2, 3, 768, 768], P(None, None, 'dp', 'mp'), may hold values from -0.21875 to 0.21875
- attn_out: bfloat16 [2, 768, 768], P(None, 'mp', 'dp'), may hold values from -0.21875 to 0.21875
- mlp_in: bfloat16 [2, 768, 3072], P(None, 'dp', 'mp'), may hold values from -0.21875 to 0.21875
- mlp_out: bfloat16 [2, 3072, 768], P(None, 'mp', 'dp'), may hold values from -0.109375 to 0.109375
- embodiment: int32 [768, 1], P('dp'), may hold values from 0 to 24; in each aligned block of 12 rows (0 to 11, 12 to 23, ...) no two rows name the same one
- levels: int32 [768, 2], P('dp'), may hold values from 0 to 19
- actions: bfloat16 [768, 2, 56], P('dp'), may hold values from -1 to 1
- noise: bfloat16 [768, 2, 56], P('dp'), may hold values from -5 to 5
- action_dims: int32 [25], replicated, may hold values from 7 to 14
- head_read: bfloat16 [64, 768, 256], P('dp'), may hold values from -0.21875 to 0.21875
- head_act: bfloat16 [64, 56, 256], P('dp'), may hold values from -0.75 to 0.75
- time_table: bfloat16 [64, 20, 256], P('dp'), may hold values from -5 to 5
- block_in: bfloat16 [64, 256, 256], P('dp'), may hold values from -0.375 to 0.375
- block_out: bfloat16 [64, 256, 256], P('dp'), may hold values from -0.375 to 0.375
- head_out: bfloat16 [64, 256, 56], P('dp'), may hold values from -0.375 to 0.375
Outputs:
- readout_grad: bfloat16 [768, 2, 768], P(('dp', 'mp'))
- grad_read: float32 [64, 768, 256], P('dp', 'mp')
- grad_act: float32 [64, 56, 256], P('dp')
- grad_time: float32 [64, 20, 256], P('dp')
- grad_block_in: float32 [64, 256, 256], P('dp')
- grad_block_out: float32 [64, 256, 256], P('dp')
- grad_head_out: float32 [64, 256, 56], P('dp')
The draws below stay inside these ranges and needn't reach their ends.
Inputs may be any that keep to these rules, and one draw needn't show every extreme that they name: Within each aligned block of 12 samples (those of one dp index) no embodiment appears twice; every embodiment appears in some block.
All inputs are finite; a program needn't handle non-finite values. No bound on the sum of `obs_mask` on one device may be relied on, other than what follows from the above.
Results may differ from the reference program's by a relative error of at most 0.024.
Values may be sent and summed in bfloat16 or wider, within the bound.
No kernel may reach another device: no remote copies, remote signals or barrier semaphores. Data moves between devices by JAX's collectives and lax.ppermute only.
A program may use at most 64 MiB of HBM per device.

```python
import math
import jax
import jax.numpy as jnp
import numpy as np
from jax import lax

D = 768
HEADS = 12
HDIM = 64
FF = 3072
HID = 256
EMB = 25
LAYERS = 2
SEQ = 64
READ = 2
LEVELS = 20
ADIM_MAX = 14
SAMP_DEV = 12
SAMPLES = 768
TOKENS = 49152
EMB_SLOTS = 64
ACT = 56
N_DP = 64
N_MP = 4


def set_ends(result, key, smallest, high):
    dims = result.shape
    place = [jax.random.randint(jax.random.fold_in(key, axis), (), 0, dims[axis]) for axis in range(len(dims))]
    result = result.at[tuple(place)].set(smallest)
    longest = dims.index(max(dims))
    place[longest] = (place[longest] + 1) % dims[longest]
    return result.at[tuple(place)].set(high)


def steps_of(rng, shape, split, least, largest):
    gain, own = 1.0, jax.random.fold_in(rng, 6)
    for axis_at, parts in split:
        draws = jnp.exp(jax.random.uniform(jax.random.fold_in(own, axis_at), (parts,), jnp.float32, least / len(split), largest / len(split)))
        gain = gain * jnp.repeat(draws, shape[axis_at] // parts).reshape([-1 if axis == axis_at else 1 for axis in range(len(shape))])
    return gain


def routed_block(rng, own, number, rows, count, top, reach, lean):
    ranking = jax.random.permutation(rng, count)
    crowded, usual = load_shares(count, rows * top, reach, lean, True), load_shares(count, rows * top, reach, lean, False)
    places = jnp.arange(count)

    def named(lengths, rotation):
        used = int((lengths > 0).sum())
        fixed = max(1, used // 4)
        shifted = fixed + (places - fixed + rotation * (used - fixed)) % max(1, count - fixed)
        return jnp.zeros((count,), jnp.int32).at[ranking[jnp.where(places < fixed, places, shifted)]].set(jnp.asarray(lengths, jnp.int32))

    lengths = jnp.where(number % 4 == 0, named(crowded, number // 4), named(usual, number - number // 4 - 1))
    mixed = jax.random.permutation(jax.random.fold_in(own, 3), count)
    donor, taker = mixed[0:count // 2 * 2:2], mixed[1:count // 2 * 2:2]
    room = jnp.minimum(lengths[donor] - 1, reach - lengths[taker]) // 2
    room = jnp.where((donor == ranking[0]) | (taker == ranking[0]) | (lengths[taker] == 0), 0, jnp.maximum(room, 0))
    shifted = jax.random.randint(jax.random.fold_in(own, 4), (count // 2,), 0, 1 << 20) % (room + 1)
    lengths = lengths.at[donor].add(-shifted).at[taker].add(shifted)
    items = jnp.searchsorted(jnp.cumsum(lengths), jnp.arange(rows * top), side="right").astype(jnp.int32)
    grid = items.reshape(top, rows).T
    grid = grid[jax.random.permutation(jax.random.fold_in(own, 1), rows)]
    rotation = jax.random.randint(jax.random.fold_in(own, 2), (rows, 1), 0, top)
    return jnp.take_along_axis(grid, (jnp.arange(top)[None, :] + rotation) % top, axis=1)


def load_shares(count, total, reach, lean, full):
    weights = [(1 << 20) // math.isqrt(grade ** lean) + 1 for grade in range(1, count + 1)]
    largest = reach if full else min(reach, max(-(-total // count), total * weights[0] // sum(weights)))
    least = 1 if total - largest >= count - 1 else 0
    counts, surplus = [largest] + [least] * (count - 1), total - largest - least * (count - 1)
    while surplus > 0:
        movable = [i for i in range(1, count) if counts[i] < largest] or [i for i in range(1, count) if counts[i] < reach]
        whole, remaining = sum([weights[i] for i in movable]), surplus
        for i in movable:
            addition = min(reach - counts[i], max(1, remaining * weights[i] // whole), surplus)
            counts[i] = counts[i] + addition
            surplus = surplus - addition
    return np.array(counts)


def bell_draw(rng, dims, scale, reach, shards=(), kind=jnp.bfloat16):
    values = scale * jax.random.normal(rng, dims, jnp.float32)
    if shards:
        values = values * steps_of(rng, dims, shards, -0.22, 0.18)
    return jnp.clip(values, -reach, reach).astype(kind)


def setup_inputs(seed: int = 0) -> dict:
    arg_keys = jax.random.split(jax.random.key(seed), 19)
    tokens = bell_draw(arg_keys[0], (TOKENS, D), 1.0, 6.0, ((0, 256),))
    obs_mask = set_ends((jax.random.randint(arg_keys[1], (SAMPLES, SEQ), 0, 4) < 3).astype(jnp.int32), jax.random.fold_in(arg_keys[1], 1), 0, 1)
    norm_gains = jnp.clip(1.0 + 0.18 * jax.random.normal(arg_keys[2], (2 * LAYERS + 1, D), jnp.float32), 0.1, 1.9)
    attn_in = bell_draw(arg_keys[3], (LAYERS, 3, D, D), D ** -0.5, 0.21875, ((2, 64), (3, 4)))
    attn_out = bell_draw(arg_keys[4], (LAYERS, D, D), D ** -0.5, 0.21875, ((1, 4), (2, 64)))
    mlp_in = bell_draw(arg_keys[5], (LAYERS, D, FF), D ** -0.5, 0.21875, ((1, 64), (2, 4)))
    mlp_out = bell_draw(arg_keys[6], (LAYERS, FF, D), FF ** -0.5, 0.109375, ((1, 4), (2, 64)))
    embodiment_keys = jax.random.split(jax.random.fold_in(arg_keys[7], 1), SAMPLES // SAMP_DEV)
    embodiment_turns = jax.random.permutation(jax.random.fold_in(arg_keys[7], 3), SAMPLES // SAMP_DEV)
    embodiment = jax.vmap(lambda own, number: routed_block(jax.random.fold_in(arg_keys[7], 2), own, number, SAMP_DEV, EMB, 1, 1, 2))(embodiment_keys, embodiment_turns).reshape((SAMPLES, 1))
    levels = set_ends(jax.random.randint(arg_keys[8], (SAMPLES, READ), 0, LEVELS), jax.random.fold_in(arg_keys[8], 1), 0, LEVELS - 1).astype(jnp.int32)
    actions = jnp.clip(jax.random.uniform(arg_keys[9], (SAMPLES, READ, ACT), jnp.float32, -1.0, 1.0) * steps_of(arg_keys[9], (SAMPLES, READ, ACT), ((0, 64),), -0.4, 0.0), -1.0, 1.0).astype(jnp.bfloat16)
    noise = bell_draw(arg_keys[10], (SAMPLES, READ, ACT), 1.0, 5.0, ((0, 64),))
    action_dims = set_ends(jax.random.randint(arg_keys[11], (EMB,), 7, ADIM_MAX + 1), jax.random.fold_in(arg_keys[11], 1), 7, ADIM_MAX).astype(jnp.int32)
    head_read = bell_draw(arg_keys[12], (EMB_SLOTS, D, HID), D ** -0.5, 0.21875, ((0, 64),))
    head_act = bell_draw(arg_keys[13], (EMB_SLOTS, ACT, HID), ACT ** -0.5, 0.75, ((0, 64),))
    time_table = bell_draw(arg_keys[14], (EMB_SLOTS, LEVELS, HID), 1.0, 5.0, ((0, 64),))
    block_in = bell_draw(arg_keys[15], (EMB_SLOTS, HID, HID), HID ** -0.5, 0.375, ((0, 64),))
    block_out = bell_draw(arg_keys[16], (EMB_SLOTS, HID, HID), HID ** -0.5, 0.375, ((0, 64),))
    head_out = bell_draw(arg_keys[17], (EMB_SLOTS, HID, ACT), HID ** -0.5, 0.375, ((0, 64),))
    return {"tokens": tokens, "obs_mask": obs_mask, "norm_gains": norm_gains, "attn_in": attn_in, "attn_out": attn_out, "mlp_in": mlp_in, "mlp_out": mlp_out, "embodiment": embodiment, "levels": levels, "actions": actions, "noise": noise, "action_dims": action_dims, "head_read": head_read, "head_act": head_act, "time_table": time_table, "block_in": block_in, "block_out": block_out, "head_out": head_out}


norm_eps = 1e-05

def normalize(values, scale_gain):
    center = values - lax.optimization_barrier(jnp.mean(values, axis=-1, keepdims=True))
    spread = lax.optimization_barrier(jnp.mean(center * center, axis=-1, keepdims=True))
    return center * lax.rsqrt(spread + norm_eps) * scale_gain

def allowed_keys(observed):
    length = observed.shape[1]
    position = jnp.arange(length)
    visible = (observed == 1) & (position < length - READ)[None, :]
    itself = position[:, None] == position[None, :]
    return visible[:, None, :] | itself[None, :, :]

def attend(queries, key_rows, value_rows, allowed):
    scores = jnp.einsum('sqhd,skhd->shqk', queries.astype(jnp.float32), key_rows.astype(jnp.float32)) * HDIM ** (-0.5)
    weights = jnp.where(allowed[:, None, :, :], jnp.exp(scores), 0.0)
    shares = (weights / lax.optimization_barrier(jnp.sum(weights, axis=-1, keepdims=True))).astype(jnp.bfloat16)
    context = jnp.einsum('shqk,skhd->sqhd', shares.astype(jnp.float32), value_rows.astype(jnp.float32))
    return context.astype(jnp.bfloat16)

def split_sum(left_side, right_side, groups):
    part_width = left_side.shape[1] // groups
    summed = jnp.zeros((left_side.shape[0], right_side.shape[1]), jnp.float32)
    for part_index in range(groups):
        lower = part_index * part_width
        partial_value = jnp.dot(left_side[:, lower:lower + part_width], right_side[lower:lower + part_width], preferred_element_type=jnp.float32)
        summed = summed + lax.optimization_barrier(partial_value.astype(jnp.bfloat16)).astype(jnp.float32)
    return summed

def trunk_block(inputs, observed, norm_gains, attn_in, attn_out, mlp_in, mlp_out):
    residual = inputs.astype(jnp.float32)
    allowed = allowed_keys(observed)
    samples = observed.shape[0]
    for layer_index in range(LAYERS):
        normed = normalize(residual, norm_gains[2 * layer_index]).astype(jnp.bfloat16)
        projected = [jnp.dot(normed, attn_in[layer_index, member], preferred_element_type=jnp.float32).astype(jnp.bfloat16).reshape(samples, SEQ, HEADS, HDIM) for member in range(3)]
        context = attend(projected[0], projected[1], projected[2], allowed).reshape(-1, D)
        residual = residual + split_sum(context, attn_out[layer_index], N_MP)
        normed = normalize(residual, norm_gains[2 * layer_index + 1]).astype(jnp.bfloat16)
        hidden = jax.nn.gelu(jnp.dot(normed, mlp_in[layer_index], preferred_element_type=jnp.float32), approximate=True).astype(jnp.bfloat16)
        residual = residual + split_sum(hidden, mlp_out[layer_index], N_MP)
    ending = residual.reshape(samples, SEQ, D)[:, SEQ - READ:, :]
    return normalize(ending, norm_gains[2 * LAYERS]).astype(jnp.bfloat16)

def plan():
    steps_up = (jnp.arange(LEVELS, dtype=jnp.float32) + 1.0) / LEVELS
    anchor = math.cos(0.008 / 1.008 * math.pi / 2) ** 2
    return jnp.cos((steps_up + 0.008) / 1.008 * (math.pi / 2)) ** 2 / anchor

def noisy_pair(level_ids, clean, noise_draw, table):
    picked = (level_ids[..., None] == jnp.arange(LEVELS)).astype(jnp.float32)
    kept = lax.optimization_barrier(jnp.sum(picked * table, axis=-1))[..., None]
    mixed = jnp.sqrt(kept) * clean.astype(jnp.float32) + jnp.sqrt(1.0 - kept) * noise_draw.astype(jnp.float32)
    return mixed.astype(jnp.bfloat16)

def tail(first, target, weight_mask, inner_weight, outer_weight, final_weight):
    highest = lax.Precision.HIGHEST
    active = jax.nn.silu(first).astype(jnp.bfloat16)
    inner = jnp.dot(active, inner_weight, preferred_element_type=jnp.float32, precision=highest)
    second = jax.nn.silu(inner).astype(jnp.bfloat16)
    hidden = first + jnp.dot(second, outer_weight, preferred_element_type=jnp.float32, precision=highest)
    third = jax.nn.silu(hidden).astype(jnp.bfloat16)
    predicted = jnp.dot(third, final_weight, preferred_element_type=jnp.float32, precision=highest)
    differ = predicted - target
    return 0.5 * jnp.sum(weight_mask * differ * differ)

def reference(tokens, obs_mask, norm_gains, attn_in, attn_out, mlp_in, mlp_out, embodiment, levels, actions, noise, action_dims, head_read, head_act, time_table, block_in, block_out, head_out):

    def one_block(pieces):
        return trunk_block(pieces[0], pieces[1], norm_gains, attn_in, attn_out, mlp_in, mlp_out)
    blocks = lax.map(one_block, (tokens.reshape(N_DP, SAMP_DEV * SEQ, D), obs_mask.reshape(N_DP, SAMP_DEV, SEQ)))
    readouts = blocks.reshape(-1, D)
    table = plan()
    noisy = noisy_pair(levels, actions, noise, table).reshape(-1, ACT)
    target = noise.reshape(-1, ACT).astype(jnp.float32)
    level_rows = levels.reshape(-1)
    owner_rows = jnp.repeat(embodiment[:, 0], READ)
    one_hot = (level_rows[:, None] == jnp.arange(LEVELS)).astype(jnp.bfloat16)
    column = jnp.arange(ACT) % ADIM_MAX
    slot_count = head_read.shape[0]

    def per_head(carried, slot):
        read_weight = head_read[slot]
        live = (owner_rows == slot).astype(jnp.float32)
        dims_here = jnp.sum(jnp.where(jnp.arange(EMB) == slot, action_dims, 0))
        weight_mask = live[:, None] * (column[None, :] < dims_here).astype(jnp.float32)
        first = jnp.dot(readouts, read_weight, preferred_element_type=jnp.float32)
        first = first + jnp.dot(noisy, head_act[slot], preferred_element_type=jnp.float32)
        first = first + jnp.dot(one_hot, time_table[slot], preferred_element_type=jnp.float32)

        def head_loss(first_in, inner_weight, outer_weight, final_weight):
            return tail(first_in, target, weight_mask, inner_weight, outer_weight, final_weight)
        loss_value, pullback = jax.vjp(head_loss, first, block_in[slot].astype(jnp.float32), block_out[slot].astype(jnp.float32), head_out[slot].astype(jnp.float32))
        grad_first, grad_inner, grad_outer, grad_final = pullback(jnp.ones((), jnp.float32))
        grad_bf = grad_first.astype(jnp.bfloat16)
        grad_readin = jnp.dot(readouts.T, grad_bf, preferred_element_type=jnp.float32)
        grad_actin = jnp.dot(noisy.T, grad_bf, preferred_element_type=jnp.float32)
        grad_timein = jnp.dot(one_hot.T, grad_bf, preferred_element_type=jnp.float32)
        carried = carried + jnp.dot(grad_bf, read_weight.T, preferred_element_type=jnp.float32)
        return (carried, (grad_readin, grad_actin, grad_timein, grad_inner, grad_outer, grad_final))
    returned, grads = lax.scan(per_head, jnp.zeros(readouts.shape, jnp.float32), jnp.arange(slot_count))
    grad_readin, grad_actin, grad_timein, grad_inner, grad_outer, grad_final = grads
    return (returned.astype(jnp.bfloat16).reshape(SAMPLES, READ, D), grad_readin, grad_actin, grad_timein, grad_inner, grad_outer, grad_final)
```

```python
import math

import jax
import jax.numpy as jnp
from jax import lax
from jax.sharding import Mesh, PartitionSpec as P

D = 768
HDIM = 64
EMB = 25
READ = 2
LEVELS = 20
ADIM_MAX = 14
ACT = 56
SEQ = 64
F32 = jnp.float32
BF16 = jnp.bfloat16
DP = ("z", "y", "c")


norm_eps = 1e-05


def sent_to_all(x, axis):
    copies = jnp.broadcast_to(x, (lax.axis_size(axis), *x.shape))
    return lax.all_to_all(copies, axis, split_axis=0, concat_axis=0, tiled=True)


def gather_rows(x, axis):
    pieces = sent_to_all(x, axis)
    return pieces.reshape(-1, *x.shape[1:])


def summed_on_arrival(x, axis):
    pieces = x.reshape(lax.axis_size(axis), -1, x.shape[1])
    arrived = lax.all_to_all(pieces, axis, split_axis=0, concat_axis=0, tiled=True)
    return arrived.astype(F32).sum(axis=0)


def summed_for_all(x, axis):
    return sent_to_all(x, axis).astype(F32).sum(axis=0)


def gather_turned(arrays, axis, dims):
    turned = [jnp.moveaxis(a, dim, 0) for a, dim in zip(arrays, dims)]
    widths = [t[0].size for t in turned]
    both = jnp.concatenate([t.reshape(-1, w) for t, w in zip(turned, widths)], axis=1)
    whole = lax.all_gather(both, axis, axis=0, tiled=True)
    pieces = jnp.split(whole, [sum(widths[:k]) for k in range(1, len(widths))], axis=1)
    return tuple(
        (
            jnp.moveaxis(b.reshape(-1, *t.shape[1:]), 0, dim)
            for b, t, dim in zip(pieces, turned, dims)
        )
    )


def normalize(values, scale_gain):
    center = values - jnp.mean(values, axis=-1, keepdims=True)
    spread = jnp.mean(center * center, axis=-1, keepdims=True)
    return center * lax.rsqrt(spread + norm_eps) * scale_gain


def mm(a, b):
    return jnp.dot(a, b, preferred_element_type=F32)


def allowed_keys(observed):
    length = observed.shape[1]
    position = jnp.arange(length)
    visible = (observed == 1) & (position < length - READ)[None, :]
    itself = position[:, None] == position[None, :]
    return visible[:, None, :] | itself[None, :, :]


def attend(queries, key_rows, value_rows, allowed):
    scores = jnp.einsum(
        "sqhd,skhd->shqk", queries, key_rows, preferred_element_type=F32
    ) * HDIM ** (-0.5)
    weights = jnp.where(allowed[:, None, :, :], jnp.exp(scores), 0.0)
    shares = (weights / jnp.sum(weights, axis=-1, keepdims=True)).astype(BF16)
    context = jnp.einsum("shqk,skhd->sqhd", shares, value_rows, preferred_element_type=F32)
    return context.astype(BF16)


def plan():
    steps_up = (jnp.arange(LEVELS, dtype=F32) + 1.0) / LEVELS
    anchor = math.cos(0.008 / 1.008 * math.pi / 2) ** 2
    return jnp.cos((steps_up + 0.008) / 1.008 * (math.pi / 2)) ** 2 / anchor


def noisy_pair(level_ids, clean, noise_draw, table):
    picked = (level_ids[..., None] == jnp.arange(LEVELS)).astype(F32)
    kept = jnp.sum(picked * table, axis=-1)[..., None]
    mixed = jnp.sqrt(kept) * clean.astype(F32) + jnp.sqrt(1.0 - kept) * noise_draw.astype(F32)
    return mixed.astype(BF16)


def tail(first, target, weight_mask, inner_weight, outer_weight, final_weight):
    active = jax.nn.silu(first).astype(BF16)
    inner = jnp.dot(active, inner_weight, preferred_element_type=F32)
    second = jax.nn.silu(inner).astype(BF16)
    hidden = first + jnp.dot(second, outer_weight, preferred_element_type=F32)
    third = jax.nn.silu(hidden).astype(BF16)
    predicted = jnp.dot(third, final_weight, preferred_element_type=F32)
    differ = predicted - target
    return 0.5 * jnp.sum(weight_mask * differ * differ)


def head_grads(first, inner_weight, outer_weight, final_weight, target, weight_mask):

    def head_loss(first_in, inner_in, outer_in, final_in):
        return tail(first_in, target, weight_mask, inner_in, outer_in, final_in)

    loss_value, pullback = jax.vjp(head_loss, first, inner_weight, outer_weight, final_weight)
    return pullback(jnp.ones((), F32))


def on_device(
    tokens,
    obs_mask,
    norm_gains,
    attn_in,
    attn_out,
    mlp_in,
    mlp_out,
    embodiment,
    levels,
    actions,
    noise,
    action_dims,
    head_read,
    head_act,
    time_table,
    block_in,
    block_out,
    head_out,
):
    width = attn_in.shape[3]
    heads = width // HDIM
    peers = lax.axis_size(DP)
    my_model = lax.axis_index("mp")
    my_owner = lax.axis_index(DP)

    owners = embodiment[:, 0]
    place = (jnp.arange(peers)[:, None] == owners[None, :]).astype(BF16)
    noisy = noisy_pair(levels, actions, noise, plan())
    marks = (levels + 1).astype(BF16)[..., None]
    early = jnp.concatenate([noisy, noise, marks, jnp.zeros((*levels.shape, 15), BF16)], axis=-1)
    sent = jnp.einsum("es,srf->erf", place, early, preferred_element_type=F32).astype(BF16)
    got = lax.all_to_all(sent, DP, split_axis=0, concat_axis=0, tiled=True)
    got = got.reshape(peers * READ, 128)

    def weights_of(layer):
        return gather_turned(
            (attn_in[layer], attn_out[layer], mlp_in[layer], mlp_out[layer]), DP, (1, 1, 0, 1)
        )

    residual = tokens.astype(F32)
    normed = normalize(residual, norm_gains[0]).astype(BF16)
    gathered = gather_rows(normed, "mp")
    mask_group = gather_rows(obs_mask, "mp")
    samples = mask_group.shape[0]
    allowed = allowed_keys(mask_group)
    qkv_weight, out_weight, up_weight, down_weight = weights_of(0)
    projected = jnp.einsum("td,jdc->jtc", gathered, qkv_weight, preferred_element_type=F32)
    projected = projected.astype(BF16).reshape(3, samples, SEQ, heads, HDIM)
    context = attend(projected[0], projected[1], projected[2], allowed).reshape(-1, width)
    residual = residual + summed_on_arrival(mm(context, out_weight).astype(BF16), "mp")
    normed = normalize(residual, norm_gains[1]).astype(BF16)
    gathered = gather_rows(normed, "mp")
    hidden = jax.nn.gelu(mm(gathered, up_weight), approximate=True).astype(BF16)
    residual = residual + summed_on_arrival(mm(hidden, down_weight).astype(BF16), "mp")

    whole = gather_rows(residual.astype(BF16), "mp").astype(F32)
    qkv_weight, out_weight, up_weight, down_weight = weights_of(1)
    normed = normalize(whole, norm_gains[2]).astype(BF16)
    last = slice(SEQ - READ, SEQ)
    ending = whole.reshape(samples, SEQ, D)[:, last].reshape(-1, D)
    normed_end = normed.reshape(samples, SEQ, D)[:, last].reshape(-1, D)
    queries = mm(normed_end, qkv_weight[0]).astype(BF16).reshape(samples, READ, heads, HDIM)
    key_rows = mm(normed, qkv_weight[1]).astype(BF16).reshape(samples, SEQ, heads, HDIM)
    value_rows = mm(normed, qkv_weight[2]).astype(BF16).reshape(samples, SEQ, heads, HDIM)
    context = attend(queries, key_rows, value_rows, allowed[:, last]).reshape(-1, width)
    ending = ending + summed_for_all(mm(context, out_weight).astype(BF16), "mp")
    normed = normalize(ending, norm_gains[3]).astype(BF16)
    hidden = jax.nn.gelu(mm(normed, up_weight), approximate=True).astype(BF16)
    ending = ending + summed_for_all(mm(hidden, down_weight).astype(BF16), "mp")
    readouts = normalize(ending, norm_gains[4]).astype(BF16).reshape(samples, READ * D)

    send = mm(place, readouts).astype(BF16)
    features = lax.all_to_all(send, DP, split_axis=0, concat_axis=0, tiled=True)
    features = features.reshape(peers * READ, D)
    head_noisy = got[:, :ACT]
    head_target = got[:, ACT : 2 * ACT].astype(F32)
    head_level = got[:, 2 * ACT].astype(jnp.int32) - 1
    onehot = (head_level[:, None] == jnp.arange(LEVELS)).astype(BF16)
    dims_here = jnp.sum(jnp.where(jnp.arange(EMB) == my_owner, action_dims, 0))
    column = jnp.arange(ACT) % ADIM_MAX
    weight_mask = (head_level >= 0).astype(F32)[:, None] * (column < dims_here).astype(F32)[None, :]
    others = mm(head_noisy, head_act[0]) + mm(onehot, time_table[0])
    first = mm(features, head_read[0]) + others
    grad_first, grad_inner, grad_outer, grad_final = head_grads(
        first,
        block_in[0].astype(F32),
        block_out[0].astype(F32),
        head_out[0].astype(F32),
        head_target,
        weight_mask,
    )
    grad_bf = grad_first.astype(BF16)
    backward = jnp.einsum("nc,dc->nd", grad_bf, head_read[0], preferred_element_type=F32)
    backward = backward.astype(BF16).reshape(peers, READ * D)
    arrived = lax.all_to_all(backward, DP, split_axis=0, concat_axis=0, tiled=True)
    mine = samples // 4
    own_place = lax.dynamic_slice_in_dim(place, my_model * mine, mine, 1)
    arrived = jnp.einsum("es,ef->sf", own_place, arrived, preferred_element_type=F32)
    arrived = arrived.astype(BF16).reshape(mine, READ, D)
    part = lax.dynamic_slice_in_dim(features, my_model * width, width, 1)
    grad_read = jnp.einsum("nd,nc->dc", part, grad_bf, preferred_element_type=F32)
    grad_act = jnp.einsum("na,nc->ac", head_noisy, grad_bf, preferred_element_type=F32)
    grad_time = jnp.einsum("nl,nc->lc", onehot, grad_bf, preferred_element_type=F32)
    return (
        arrived,
        grad_read[None],
        grad_act[None],
        grad_time[None],
        grad_inner[None],
        grad_outer[None],
        grad_final[None],
    )


def solution(mesh):
    fine = Mesh(mesh.devices.reshape(8, 4, 2, 4), ("z", "y", "c", "mp"))
    both = (*DP, "mp")
    placed = (
        P(both, None),
        P(both, None),
        P(),
        P(None, None, DP, "mp"),
        P(None, "mp", DP),
        P(None, DP, "mp"),
        P(None, "mp", DP),
        P(DP, None),
        P(DP, None),
        P(DP, None, None),
        P(DP, None, None),
        P(),
        P(DP, None, None),
        P(DP, None, None),
        P(DP, None, None),
        P(DP, None, None),
        P(DP, None, None),
        P(DP, None, None),
    )
    return jax.shard_map(
        on_device,
        mesh=fine,
        in_specs=placed,
        out_specs=(
            P(both, None, None),
            P(DP, "mp", None),
            P(DP, None, None),
            P(DP, None, None),
            P(DP, None, None),
            P(DP, None, None),
            P(DP, None, None),
        ),
        check_vma=False,
    )
```

```python
import math

import jax
import jax.numpy as jnp
from jax import lax
from jax.sharding import Mesh, PartitionSpec as P

D = 768
HDIM = 64
EMB = 25
READ = 2
LEVELS = 20
ADIM_MAX = 14
ACT = 56
SEQ = 64
F32 = jnp.float32
BF16 = jnp.bfloat16
DP = ("z", "y", "c")


norm_eps = 1e-05


def sent_to_all(x, axis):
    copies = jnp.broadcast_to(x, (lax.axis_size(axis), *x.shape))
    return lax.all_to_all(copies, axis, split_axis=0, concat_axis=0, tiled=True)


def gather_rows(x, axis):
    pieces = sent_to_all(x, axis)
    return pieces.reshape(-1, *x.shape[1:])


def summed_on_arrival(x, axis):
    pieces = x.reshape(lax.axis_size(axis), -1, x.shape[1])
    arrived = lax.all_to_all(pieces, axis, split_axis=0, concat_axis=0, tiled=True)
    return arrived.astype(F32).sum(axis=0)


def summed_for_all(x, axis):
    return sent_to_all(x, axis).astype(F32).sum(axis=0)


def normalize(values, scale_gain):
    center = values - jnp.mean(values, axis=-1, keepdims=True)
    spread = jnp.mean(center * center, axis=-1, keepdims=True)
    return center * lax.rsqrt(spread + norm_eps) * scale_gain


def mm(a, b):
    return jnp.dot(a, b, preferred_element_type=F32)


def mm_t(a, b):
    return jnp.einsum("tk,dk->td", a, b, preferred_element_type=F32)


def allowed_keys(observed):
    length = observed.shape[1]
    position = jnp.arange(length)
    visible = (observed == 1) & (position < length - READ)[None, :]
    itself = position[:, None] == position[None, :]
    return visible[:, None, :] | itself[None, :, :]


def attend(queries, key_rows, value_rows, allowed):
    scores = jnp.einsum(
        "sqhd,skhd->shqk", queries, key_rows, preferred_element_type=F32
    ) * HDIM ** (-0.5)
    weights = jnp.where(allowed[:, None, :, :], jnp.exp(scores), 0.0)
    shares = (weights / jnp.sum(weights, axis=-1, keepdims=True)).astype(BF16)
    context = jnp.einsum("shqk,skhd->sqhd", shares, value_rows, preferred_element_type=F32)
    return context.astype(BF16)


def plan():
    steps_up = (jnp.arange(LEVELS, dtype=F32) + 1.0) / LEVELS
    anchor = math.cos(0.008 / 1.008 * math.pi / 2) ** 2
    return jnp.cos((steps_up + 0.008) / 1.008 * (math.pi / 2)) ** 2 / anchor


def noisy_pair(level_ids, clean, noise_draw, table):
    picked = (level_ids[..., None] == jnp.arange(LEVELS)).astype(F32)
    kept = jnp.sum(picked * table, axis=-1)[..., None]
    mixed = jnp.sqrt(kept) * clean.astype(F32) + jnp.sqrt(1.0 - kept) * noise_draw.astype(F32)
    return mixed.astype(BF16)


def tail(first, target, weight_mask, inner_weight, outer_weight, final_weight):
    active = jax.nn.silu(first).astype(BF16)
    inner = jnp.dot(active, inner_weight, preferred_element_type=F32)
    second = jax.nn.silu(inner).astype(BF16)
    hidden = first + jnp.dot(second, outer_weight, preferred_element_type=F32)
    third = jax.nn.silu(hidden).astype(BF16)
    predicted = jnp.dot(third, final_weight, preferred_element_type=F32)
    differ = predicted - target
    return 0.5 * jnp.sum(weight_mask * differ * differ)


def head_grads(first, inner_weight, outer_weight, final_weight, target, weight_mask):

    def head_loss(first_in, inner_in, outer_in, final_in):
        return tail(first_in, target, weight_mask, inner_in, outer_in, final_in)

    loss_value, pullback = jax.vjp(head_loss, first, inner_weight, outer_weight, final_weight)
    return pullback(jnp.ones((), F32))


def on_device(
    tokens,
    obs_mask,
    norm_gains,
    attn_in,
    attn_out,
    mlp_in,
    mlp_out,
    embodiment,
    levels,
    actions,
    noise,
    action_dims,
    head_read,
    head_act,
    time_table,
    block_in,
    block_out,
    head_out,
):
    width = attn_in.shape[3]
    heads = width // HDIM
    peers = lax.axis_size(DP)
    my_model = lax.axis_index("mp")
    my_owner = lax.axis_index(DP)

    own_z = lax.axis_index("z")

    full = jnp.concatenate(
        [
            jnp.moveaxis(attn_in[1], 0, 1).reshape(12, -1),
            attn_out[1].T,
            mlp_in[0],
            mlp_out[0].T,
        ],
        axis=1,
    )
    groups = full.shape[1] // width
    full = sent_to_all(full, "mp").reshape(2, 2, 12, groups, width)
    full = full.transpose(0, 2, 3, 1, 4).reshape(2, 12, -1)
    share = jnp.stack([mlp_in[1], mlp_out[1].T], axis=1).reshape(12, 2, 2, -1)
    share = share.transpose(2, 0, 1, 3).reshape(2, 12, -1)
    halves = jnp.concatenate([full, share], axis=2)
    halves = lax.all_to_all(halves, "c", split_axis=0, concat_axis=0, tiled=True)
    piece = halves.reshape(24, -1)

    owners = embodiment[:, 0]
    place = (jnp.arange(peers)[:, None] == owners[None, :]).astype(BF16)
    noisy = noisy_pair(levels, actions, noise, plan())
    marks = (levels + 1).astype(BF16)[..., None]
    early = jnp.concatenate([noisy, noise, marks, jnp.zeros((*levels.shape, 15), BF16)], axis=-1)
    sent = jnp.einsum("es,srf->erf", place, early, preferred_element_type=F32).astype(BF16)
    residual = tokens.astype(F32)
    normed = normalize(residual, norm_gains[0]).astype(BF16)
    first_piece = jnp.concatenate(
        [jnp.moveaxis(attn_in[0], 0, 1).reshape(12, -1), attn_out[0].T], axis=1
    )
    piece, sent, normed, first_piece, obs_mask = lax.optimization_barrier(
        (piece, sent, normed, first_piece, obs_mask)
    )
    gathered_weights = lax.all_gather(piece, ("c", "z", "y"), axis=0, tiled=True)

    for step in (1, 2, 4):
        other = lax.ppermute(first_piece, "z", [(k, k ^ step) for k in range(8)])
        upper = (own_z // step) % 2 == 1
        low = jnp.where(upper, other, first_piece)
        high = jnp.where(upper, first_piece, other)
        first_piece = jnp.concatenate([low, high], axis=0)
    first_weight = sent_to_all(first_piece, ("y", "c")).reshape(8, 8, 12, -1)
    first_weight = jnp.moveaxis(first_weight, 0, 1).reshape(D, -1)
    gathered = gather_rows(normed, "mp")
    mask_group = gather_rows(obs_mask, "mp")
    got = lax.all_to_all(sent, DP, split_axis=0, concat_axis=0, tiled=True)
    gathered, mask_group, got, first_weight = lax.optimization_barrier(
        (gathered, mask_group, got, first_weight)
    )
    got = got.reshape(peers * READ, 128)
    samples = mask_group.shape[0]
    projected = mm(gathered, first_weight[:, : 3 * width]).astype(BF16)
    projected = jnp.moveaxis(projected.reshape(-1, 3, width), 1, 0)
    projected = projected.reshape(3, samples, SEQ, heads, HDIM)
    context = attend(projected[0], projected[1], projected[2], allowed_keys(mask_group))
    partial_value = mm_t(context.reshape(-1, width), first_weight[:, 3 * width :])
    residual = residual + summed_on_arrival(partial_value.astype(BF16), "mp")

    residual, gathered_weights = lax.optimization_barrier((residual, gathered_weights))
    sides = gathered_weights.reshape(2, D, -1)

    def weight(side, start, columns):
        return sides[side, :, start : start + columns]

    normed = normalize(residual, norm_gains[1]).astype(BF16)
    for side in range(2):
        hidden = jax.nn.gelu(mm(normed, weight(side, 1536, 1536)), approximate=True).astype(BF16)
        residual = residual + mm_t(hidden, weight(side, 3072, 1536))
    own_samples = obs_mask.shape[0]
    normed = normalize(residual, norm_gains[2]).astype(BF16)
    last = slice(SEQ - READ, SEQ)
    ending = residual.reshape(own_samples, SEQ, D)[:, last].reshape(-1, D)
    normed_end = normed.reshape(own_samples, SEQ, D)[:, last].reshape(-1, D)
    allowed = allowed_keys(obs_mask)[:, last]
    for side in range(2):
        queries = mm(normed_end, weight(side, 0, 384)).astype(BF16)
        key_rows = mm(normed, weight(side, 384, 384)).astype(BF16)
        value_rows = mm(normed, weight(side, 768, 384)).astype(BF16)
        context = attend(
            queries.reshape(own_samples, READ, -1, HDIM),
            key_rows.reshape(own_samples, SEQ, -1, HDIM),
            value_rows.reshape(own_samples, SEQ, -1, HDIM),
            allowed,
        ).reshape(own_samples * READ, -1)
        ending = ending + mm_t(context, weight(side, 1152, 384))
    ending = gather_rows(ending.astype(BF16), "mp").astype(F32)
    normed = normalize(ending, norm_gains[3]).astype(BF16)
    partial_value = 0.0
    for side in range(2):
        hidden = jax.nn.gelu(mm(normed, weight(side, 4608, 384)), approximate=True).astype(BF16)
        partial_value = partial_value + mm_t(hidden, weight(side, 4992, 384))
    ending = ending + summed_for_all(partial_value.astype(BF16), "mp")
    readouts = normalize(ending, norm_gains[4]).astype(BF16).reshape(samples, READ * D)

    send = mm(place, readouts).astype(BF16)
    features = lax.all_to_all(send, DP, split_axis=0, concat_axis=0, tiled=True)
    features = features.reshape(peers * READ, D)
    head_noisy = got[:, :ACT]
    head_target = got[:, ACT : 2 * ACT].astype(F32)
    head_level = got[:, 2 * ACT].astype(jnp.int32) - 1
    onehot = (head_level[:, None] == jnp.arange(LEVELS)).astype(BF16)
    dims_here = jnp.sum(jnp.where(jnp.arange(EMB) == my_owner, action_dims, 0))
    column = jnp.arange(ACT) % ADIM_MAX
    weight_mask = (head_level >= 0).astype(F32)[:, None] * (column < dims_here).astype(F32)[None, :]
    others = mm(head_noisy, head_act[0]) + mm(onehot, time_table[0])
    first = mm(features, head_read[0]) + others
    grad_first, grad_inner, grad_outer, grad_final = head_grads(
        first,
        block_in[0].astype(F32),
        block_out[0].astype(F32),
        head_out[0].astype(F32),
        head_target,
        weight_mask,
    )
    grad_bf = grad_first.astype(BF16)
    backward = jnp.einsum("nc,dc->nd", grad_bf, head_read[0], preferred_element_type=F32)
    backward = backward.astype(BF16).reshape(peers, READ * D)
    arrived = lax.all_to_all(backward, DP, split_axis=0, concat_axis=0, tiled=True)
    mine = samples // 4
    own_place = lax.dynamic_slice_in_dim(place, my_model * mine, mine, 1)
    arrived = jnp.einsum("es,ef->sf", own_place, arrived, preferred_element_type=F32)
    arrived = arrived.astype(BF16).reshape(mine, READ, D)
    part = lax.dynamic_slice_in_dim(features, my_model * width, width, 1)
    grad_read = jnp.einsum("nd,nc->dc", part, grad_bf, preferred_element_type=F32)
    grad_act = jnp.einsum("na,nc->ac", head_noisy, grad_bf, preferred_element_type=F32)
    grad_time = jnp.einsum("nl,nc->lc", onehot, grad_bf, preferred_element_type=F32)
    return (
        arrived,
        grad_read[None],
        grad_act[None],
        grad_time[None],
        grad_inner[None],
        grad_outer[None],
        grad_final[None],
    )


def solution(mesh):
    fine = Mesh(mesh.devices.reshape(8, 4, 2, 4), ("z", "y", "c", "mp"))
    both = (*DP, "mp")
    placed = (
        P(both, None),
        P(both, None),
        P(),
        P(None, None, DP, "mp"),
        P(None, "mp", DP),
        P(None, DP, "mp"),
        P(None, "mp", DP),
        P(DP, None),
        P(DP, None),
        P(DP, None, None),
        P(DP, None, None),
        P(),
        P(DP, None, None),
        P(DP, None, None),
        P(DP, None, None),
        P(DP, None, None),
        P(DP, None, None),
        P(DP, None, None),
    )
    return jax.shard_map(
        on_device,
        mesh=fine,
        in_specs=placed,
        out_specs=(
            P(both, None, None),
            P(DP, "mp", None),
            P(DP, None, None),
            P(DP, None, None),
            P(DP, None, None),
            P(DP, None, None),
            P(DP, None, None),
        ),
        check_vma=False,
    )
```

```python
import math

import jax
import jax.numpy as jnp
from jax import lax
from jax.sharding import Mesh, PartitionSpec as P

D = 768
HDIM = 64
EMB = 25
READ = 2
LEVELS = 20
ADIM_MAX = 14
ACT = 56
SEQ = 64
F32 = jnp.float32
BF16 = jnp.bfloat16
DP = ("z", "y", "c")


norm_eps = 1e-05


def sent_to_all(x, axis):
    copies = jnp.broadcast_to(x, (lax.axis_size(axis), *x.shape))
    return lax.all_to_all(copies, axis, split_axis=0, concat_axis=0, tiled=True)


def gather_rows(x, axis):
    pieces = sent_to_all(x, axis)
    return pieces.reshape(-1, *x.shape[1:])


def summed_on_arrival(x, axis):
    pieces = x.reshape(lax.axis_size(axis), -1, x.shape[1])
    arrived = lax.all_to_all(pieces, axis, split_axis=0, concat_axis=0, tiled=True)
    return arrived.astype(F32).sum(axis=0)


def summed_for_all(x, axis):
    return sent_to_all(x, axis).astype(F32).sum(axis=0)


def normalize(values, scale_gain):
    center = values - jnp.mean(values, axis=-1, keepdims=True)
    spread = jnp.mean(center * center, axis=-1, keepdims=True)
    return center * lax.rsqrt(spread + norm_eps) * scale_gain


def mm(a, b):
    return jnp.dot(a, b, preferred_element_type=F32)


def mm_t(a, b):
    return jnp.einsum("tk,dk->td", a, b, preferred_element_type=F32)


def allowed_keys(observed):
    length = observed.shape[1]
    position = jnp.arange(length)
    visible = (observed == 1) & (position < length - READ)[None, :]
    itself = position[:, None] == position[None, :]
    return visible[:, None, :] | itself[None, :, :]


def attend(queries, key_rows, value_rows, allowed):
    scores = jnp.einsum(
        "sqhd,skhd->shqk", queries, key_rows, preferred_element_type=F32
    ) * HDIM ** (-0.5)
    weights = jnp.where(allowed[:, None, :, :], jnp.exp(scores), 0.0)
    shares = (weights / jnp.sum(weights, axis=-1, keepdims=True)).astype(BF16)
    context = jnp.einsum("shqk,skhd->sqhd", shares, value_rows, preferred_element_type=F32)
    return context.astype(BF16)


def plan():
    steps_up = (jnp.arange(LEVELS, dtype=F32) + 1.0) / LEVELS
    anchor = math.cos(0.008 / 1.008 * math.pi / 2) ** 2
    return jnp.cos((steps_up + 0.008) / 1.008 * (math.pi / 2)) ** 2 / anchor


def noisy_pair(level_ids, clean, noise_draw, table):
    picked = (level_ids[..., None] == jnp.arange(LEVELS)).astype(F32)
    kept = jnp.sum(picked * table, axis=-1)[..., None]
    mixed = jnp.sqrt(kept) * clean.astype(F32) + jnp.sqrt(1.0 - kept) * noise_draw.astype(F32)
    return mixed.astype(BF16)


def tail(first, target, weight_mask, inner_weight, outer_weight, final_weight):
    active = jax.nn.silu(first).astype(BF16)
    inner = jnp.dot(active, inner_weight, preferred_element_type=F32)
    second = jax.nn.silu(inner).astype(BF16)
    hidden = first + jnp.dot(second, outer_weight, preferred_element_type=F32)
    third = jax.nn.silu(hidden).astype(BF16)
    predicted = jnp.dot(third, final_weight, preferred_element_type=F32)
    differ = predicted - target
    return 0.5 * jnp.sum(weight_mask * differ * differ)


def head_grads(first, inner_weight, outer_weight, final_weight, target, weight_mask):

    def head_loss(first_in, inner_in, outer_in, final_in):
        return tail(first_in, target, weight_mask, inner_in, outer_in, final_in)

    loss_value, pullback = jax.vjp(head_loss, first, inner_weight, outer_weight, final_weight)
    return pullback(jnp.ones((), F32))


def on_device(
    tokens,
    obs_mask,
    norm_gains,
    attn_in,
    attn_out,
    mlp_in,
    mlp_out,
    embodiment,
    levels,
    actions,
    noise,
    action_dims,
    head_read,
    head_act,
    time_table,
    block_in,
    block_out,
    head_out,
):
    width = attn_in.shape[3]
    heads = width // HDIM
    peers = lax.axis_size(DP)
    my_model = lax.axis_index("mp")
    my_owner = lax.axis_index(DP)

    full = jnp.concatenate(
        [
            jnp.moveaxis(attn_in[1], 0, 1).reshape(12, -1),
            attn_out[1].T,
            mlp_in[0],
            mlp_out[0].T,
        ],
        axis=1,
    )
    groups = full.shape[1] // width
    full = sent_to_all(full, "mp").reshape(2, 2, 12, groups, width)
    full = full.transpose(0, 2, 3, 1, 4).reshape(2, 12, -1)
    share = jnp.stack([mlp_in[1], mlp_out[1].T], axis=1).reshape(12, 2, 2, -1)
    share = share.transpose(2, 0, 1, 3).reshape(2, 12, -1)
    halves = jnp.concatenate([full, share], axis=2)
    halves = lax.all_to_all(halves, "c", split_axis=0, concat_axis=0, tiled=True)
    piece = halves.reshape(24, -1)

    owners = embodiment[:, 0]
    place = (jnp.arange(peers)[:, None] == owners[None, :]).astype(BF16)
    noisy = noisy_pair(levels, actions, noise, plan())
    marks = (levels + 1).astype(BF16)[..., None]
    early = jnp.concatenate([noisy, noise, marks, jnp.zeros((*levels.shape, 15), BF16)], axis=-1)
    sent = jnp.einsum("es,srf->erf", place, early, preferred_element_type=F32).astype(BF16)
    residual = tokens.astype(F32)
    normed = normalize(residual, norm_gains[0]).astype(BF16)
    mask_row = jnp.pad(obs_mask.reshape(1, -1).astype(BF16), ((0, 15), (0, D - obs_mask.size)))
    rows = jnp.concatenate([normed, mask_row], axis=0)
    first_piece = jnp.concatenate(
        [jnp.moveaxis(attn_in[0], 0, 1).reshape(12, -1), attn_out[0].T], axis=1
    )
    piece, rows = lax.optimization_barrier((piece, rows))
    gathered_weights = lax.all_gather(piece, ("c", "z", "y"), axis=0, tiled=True)

    for axis, step in (("z", 1), ("z", 2), ("z", 4), ("y", 1), ("y", 2), ("c", 1)):
        swapped = [(k, k ^ step) for k in range(lax.axis_size(axis))]
        other = lax.ppermute(first_piece, axis, swapped)
        upper = (lax.axis_index(axis) // step) % 2 == 1
        low = jnp.where(upper, other, first_piece)
        high = jnp.where(upper, first_piece, other)
        first_piece = jnp.concatenate([low, high], axis=0)
    first_weight = first_piece.reshape(2, 4, 8, 12, -1).transpose(2, 1, 0, 3, 4).reshape(D, -1)
    arrived = sent_to_all(rows, "mp")
    own_rows = normed.shape[0]
    gathered = arrived[:, :own_rows].reshape(-1, D)
    mask_group = arrived[:, own_rows, :own_rows].astype(jnp.int32).reshape(-1, SEQ)
    samples = mask_group.shape[0]
    projected = mm(gathered, first_weight[:, : 3 * width]).astype(BF16)
    projected = jnp.moveaxis(projected.reshape(-1, 3, width), 1, 0)
    projected = projected.reshape(3, samples, SEQ, heads, HDIM)
    context = attend(projected[0], projected[1], projected[2], allowed_keys(mask_group))
    partial_value = mm_t(context.reshape(-1, width), first_weight[:, 3 * width :])
    partial_value, sent = lax.optimization_barrier((partial_value.astype(BF16), sent))
    residual = residual + summed_on_arrival(partial_value, "mp")
    got = lax.all_to_all(sent, DP, split_axis=0, concat_axis=0, tiled=True)
    got = got.reshape(peers * READ, 128)

    residual, got, gathered_weights = lax.optimization_barrier((residual, got, gathered_weights))
    sides = gathered_weights.reshape(2, D, -1)

    def weight(side, start, columns):
        return sides[side, :, start : start + columns]

    normed = normalize(residual, norm_gains[1]).astype(BF16)
    for side in range(2):
        hidden = jax.nn.gelu(mm(normed, weight(side, 1536, 1536)), approximate=True).astype(BF16)
        residual = residual + mm_t(hidden, weight(side, 3072, 1536))
    own_samples = obs_mask.shape[0]
    normed = normalize(residual, norm_gains[2]).astype(BF16)
    last = slice(SEQ - READ, SEQ)
    ending = residual.reshape(own_samples, SEQ, D)[:, last].reshape(-1, D)
    normed_end = normed.reshape(own_samples, SEQ, D)[:, last].reshape(-1, D)
    allowed = allowed_keys(obs_mask)[:, last]
    for side in range(2):
        queries = mm(normed_end, weight(side, 0, 384)).astype(BF16)
        key_rows = mm(normed, weight(side, 384, 384)).astype(BF16)
        value_rows = mm(normed, weight(side, 768, 384)).astype(BF16)
        context = attend(
            queries.reshape(own_samples, READ, -1, HDIM),
            key_rows.reshape(own_samples, SEQ, -1, HDIM),
            value_rows.reshape(own_samples, SEQ, -1, HDIM),
            allowed,
        ).reshape(own_samples * READ, -1)
        ending = ending + mm_t(context, weight(side, 1152, 384))
    ending = gather_rows(ending.astype(BF16), "mp").astype(F32)
    normed = normalize(ending, norm_gains[3]).astype(BF16)
    partial_value = 0.0
    for side in range(2):
        hidden = jax.nn.gelu(mm(normed, weight(side, 4608, 384)), approximate=True).astype(BF16)
        partial_value = partial_value + mm_t(hidden, weight(side, 4992, 384))
    ending = ending + summed_for_all(partial_value.astype(BF16), "mp")
    readouts = normalize(ending, norm_gains[4]).astype(BF16).reshape(samples, READ * D)

    send = mm(place, readouts).astype(BF16)
    features = lax.all_to_all(send, DP, split_axis=0, concat_axis=0, tiled=True)
    features = features.reshape(peers * READ, D)
    head_noisy = got[:, :ACT]
    head_target = got[:, ACT : 2 * ACT].astype(F32)
    head_level = got[:, 2 * ACT].astype(jnp.int32) - 1
    onehot = (head_level[:, None] == jnp.arange(LEVELS)).astype(BF16)
    dims_here = jnp.sum(jnp.where(jnp.arange(EMB) == my_owner, action_dims, 0))
    column = jnp.arange(ACT) % ADIM_MAX
    weight_mask = (head_level >= 0).astype(F32)[:, None] * (column < dims_here).astype(F32)[None, :]
    others = mm(head_noisy, head_act[0]) + mm(onehot, time_table[0])
    first = mm(features, head_read[0]) + others
    grad_first, grad_inner, grad_outer, grad_final = head_grads(
        first,
        block_in[0].astype(F32),
        block_out[0].astype(F32),
        head_out[0].astype(F32),
        head_target,
        weight_mask,
    )
    grad_bf = grad_first.astype(BF16)
    backward = jnp.einsum("nc,dc->nd", grad_bf, head_read[0], preferred_element_type=F32)
    backward = backward.astype(BF16).reshape(peers, READ * D)
    arrived = lax.all_to_all(backward, DP, split_axis=0, concat_axis=0, tiled=True)
    mine = samples // 4
    own_place = lax.dynamic_slice_in_dim(place, my_model * mine, mine, 1)
    arrived = jnp.einsum("es,ef->sf", own_place, arrived, preferred_element_type=F32)
    arrived = arrived.astype(BF16).reshape(mine, READ, D)
    part = lax.dynamic_slice_in_dim(features, my_model * width, width, 1)
    grad_read = jnp.einsum("nd,nc->dc", part, grad_bf, preferred_element_type=F32)
    grad_act = jnp.einsum("na,nc->ac", head_noisy, grad_bf, preferred_element_type=F32)
    grad_time = jnp.einsum("nl,nc->lc", onehot, grad_bf, preferred_element_type=F32)
    return (
        arrived,
        grad_read[None],
        grad_act[None],
        grad_time[None],
        grad_inner[None],
        grad_outer[None],
        grad_final[None],
    )


def solution(mesh):
    fine = Mesh(mesh.devices.reshape(8, 4, 2, 4), ("z", "y", "c", "mp"))
    both = (*DP, "mp")
    placed = (
        P(both, None),
        P(both, None),
        P(),
        P(None, None, DP, "mp"),
        P(None, "mp", DP),
        P(None, DP, "mp"),
        P(None, "mp", DP),
        P(DP, None),
        P(DP, None),
        P(DP, None, None),
        P(DP, None, None),
        P(),
        P(DP, None, None),
        P(DP, None, None),
        P(DP, None, None),
        P(DP, None, None),
        P(DP, None, None),
        P(DP, None, None),
    )
    return jax.shard_map(
        on_device,
        mesh=fine,
        in_specs=placed,
        out_specs=(
            P(both, None, None),
            P(DP, "mp", None),
            P(DP, None, None),
            P(DP, None, None),
            P(DP, None, None),
            P(DP, None, None),
            P(DP, None, None),
        ),
        check_vma=False,
    )
```

```python
import math

import jax
import jax.numpy as jnp
from jax import lax
from jax.experimental import pallas as pl
from jax.experimental.pallas import tpu as pltpu
from jax.sharding import Mesh, PartitionSpec as P

D = 768
HDIM = 64
EMB = 25
READ = 2
LEVELS = 20
ADIM_MAX = 14
ACT = 56
SEQ = 64
F32 = jnp.float32
BF16 = jnp.bfloat16
DP = ("z", "y", "c")


norm_eps = 1e-05


def sent_to_all(x, axis):
    copies = jnp.broadcast_to(x, (lax.axis_size(axis), *x.shape))
    return lax.all_to_all(copies, axis, split_axis=0, concat_axis=0, tiled=True)


def gather_rows(x, axis):
    pieces = sent_to_all(x, axis)
    return pieces.reshape(-1, *x.shape[1:])


def summed_on_arrival(x, axis):
    pieces = x.reshape(lax.axis_size(axis), -1, x.shape[1])
    arrived = lax.all_to_all(pieces, axis, split_axis=0, concat_axis=0, tiled=True)
    return arrived.astype(F32).sum(axis=0)


def summed_for_all(x, axis):
    return sent_to_all(x, axis).astype(F32).sum(axis=0)


def normalize(values, scale_gain):
    center = values - jnp.mean(values, axis=-1, keepdims=True)
    spread = jnp.mean(center * center, axis=-1, keepdims=True)
    return center * lax.rsqrt(spread + norm_eps) * scale_gain


def mm(a, b):
    return jnp.dot(a, b, preferred_element_type=F32)


def mm_t(a, b):
    return jnp.einsum("tk,dk->td", a, b, preferred_element_type=F32)


def allowed_keys(observed):
    length = observed.shape[1]
    position = jnp.arange(length)
    visible = (observed == 1) & (position < length - READ)[None, :]
    itself = position[:, None] == position[None, :]
    return visible[:, None, :] | itself[None, :, :]


def attend(queries, key_rows, value_rows, allowed):
    scores = jnp.einsum(
        "sqhd,skhd->shqk", queries, key_rows, preferred_element_type=F32
    ) * HDIM ** (-0.5)
    weights = jnp.where(allowed[:, None, :, :], jnp.exp(scores), 0.0)
    shares = (weights / jnp.sum(weights, axis=-1, keepdims=True)).astype(BF16)
    context = jnp.einsum("shqk,skhd->sqhd", shares, value_rows, preferred_element_type=F32)
    return context.astype(BF16)


def nt(a, b):
    return lax.dot_general(a, b, (((1,), (1,)), ((), ())), preferred_element_type=F32)


def trunk_rows_kernel(res_ref, mask_ref, gain_ref, all_ref, out_ref, mlp, att, mlp_sem, att_sem):
    def block(side, part):
        return pltpu.make_async_copy(
            all_ref.at[pl.ds(side * D, D), pl.ds(1536 * (part + 1), 1536)],
            mlp.at[side, part],
            mlp_sem.at[side, part],
        )

    def attention(side):
        return pltpu.make_async_copy(
            all_ref.at[pl.ds(side * D, D), pl.ds(0, 1536)], att.at[side], att_sem.at[side]
        )

    for side in range(2):
        for part in range(2):
            block(side, part).start()
    for side in range(2):
        attention(side).start()
    residual = res_ref[...]
    normed = normalize(residual, gain_ref[1:2, :]).astype(BF16)
    for side in range(2):
        block(side, 0).wait()
        hidden = jax.nn.gelu(mm(normed, mlp[side, 0]), approximate=True).astype(BF16)
        block(side, 1).wait()
        residual = residual + nt(hidden, mlp[side, 1])
    normed = normalize(residual, gain_ref[2:3, :])
    ends = [residual[SEQ * k + SEQ - READ : SEQ * (k + 1)] for k in (0, 1, 2, 2)]
    ending = jnp.concatenate(ends, axis=0)
    ends = [normed[SEQ * k + SEQ - READ : SEQ * (k + 1)] for k in (0, 1, 2, 2)]
    normed_end = jnp.concatenate(ends, axis=0).astype(BF16)
    normed = normed.astype(BF16)
    rows, keys, width = 48, residual.shape[0], 384
    row = lax.broadcasted_iota(jnp.int32, (rows, keys), 0) % 8
    key = lax.broadcasted_iota(jnp.int32, (rows, keys), 1)
    place = key % SEQ
    seen = (mask_ref[...] == 1) & (place < SEQ - READ)
    allowed = (key // SEQ == jnp.minimum(row // READ, 2)) & (
        seen | (place == SEQ - READ + row % READ)
    )
    own_head = (
        lax.broadcasted_iota(jnp.int32, (rows, width), 0) // 8
        == lax.broadcasted_iota(jnp.int32, (rows, width), 1) // HDIM
    )
    for side in range(2):
        attention(side).wait()
        queries = mm(normed_end, att[side, :, 0:384]).astype(BF16).astype(F32)
        key_rows = mm(normed, att[side, :, 384:768]).astype(BF16)
        value_rows = mm(normed, att[side, :, 768:1152]).astype(BF16)
        spread = jnp.where(own_head, jnp.concatenate([queries] * 6, axis=0), 0.0).astype(BF16)
        scores = nt(spread, key_rows) * HDIM ** (-0.5)
        weights = jnp.where(allowed, jnp.exp(scores), 0.0)
        shares = (weights / jnp.sum(weights, axis=-1, keepdims=True)).astype(BF16)
        context = jnp.where(own_head, mm(shares, value_rows), 0.0)
        context = sum(context[8 * k : 8 * k + 8] for k in range(6)).astype(BF16)
        ending = ending + nt(context, att[side, :, 1152:1536])
    out_ref[...] = ending.astype(BF16)


def trunk_rows(residual, mask_row, gains, weights):
    vmem = pl.BlockSpec(memory_space=pltpu.VMEM)
    return pl.pallas_call(
        trunk_rows_kernel,
        out_shape=jax.ShapeDtypeStruct((8, D), BF16),
        in_specs=[vmem, vmem, vmem, pl.BlockSpec(memory_space=pl.ANY)],
        out_specs=vmem,
        scratch_shapes=[
            pltpu.VMEM((2, 2, D, 1536), BF16),
            pltpu.VMEM((2, D, 1536), BF16),
            pltpu.SemaphoreType.DMA((2, 2)),
            pltpu.SemaphoreType.DMA((2,)),
        ],
        compiler_params=pltpu.CompilerParams(vmem_limit_bytes=40 * 1024 * 1024),
        name="trunk_rows",
    )(residual, mask_row, gains, weights)


def readout_mlp_kernel(end_ref, gain_ref, all_ref, out_ref, mlp, sem):
    def block(side):
        return pltpu.make_async_copy(
            all_ref.at[pl.ds(side * D, D), pl.ds(4608, 768)], mlp.at[side], sem.at[side]
        )

    for side in range(2):
        block(side).start()
    normed = normalize(end_ref[...].astype(F32), gain_ref[3:4, :]).astype(BF16)
    total = jnp.zeros(end_ref.shape, F32)
    for side in range(2):
        block(side).wait()
        hidden = jax.nn.gelu(mm(normed, mlp[side, :, 0:384]), approximate=True).astype(BF16)
        total = total + nt(hidden, mlp[side, :, 384:768])
    out_ref[...] = total.astype(BF16)


def readout_mlp(ending, gains, weights):
    vmem = pl.BlockSpec(memory_space=pltpu.VMEM)
    return pl.pallas_call(
        readout_mlp_kernel,
        out_shape=jax.ShapeDtypeStruct(ending.shape, BF16),
        in_specs=[vmem, vmem, pl.BlockSpec(memory_space=pl.ANY)],
        out_specs=vmem,
        scratch_shapes=[pltpu.VMEM((2, D, 768), BF16), pltpu.SemaphoreType.DMA((2,))],
        name="readout_mlp",
    )(ending, gains, weights)


def plan():
    steps_up = (jnp.arange(LEVELS, dtype=F32) + 1.0) / LEVELS
    anchor = math.cos(0.008 / 1.008 * math.pi / 2) ** 2
    return jnp.cos((steps_up + 0.008) / 1.008 * (math.pi / 2)) ** 2 / anchor


def noisy_pair(level_ids, clean, noise_draw, table):
    picked = (level_ids[..., None] == jnp.arange(LEVELS)).astype(F32)
    kept = jnp.sum(picked * table, axis=-1)[..., None]
    mixed = jnp.sqrt(kept) * clean.astype(F32) + jnp.sqrt(1.0 - kept) * noise_draw.astype(F32)
    return mixed.astype(BF16)


def tail(first, target, weight_mask, inner_weight, outer_weight, final_weight):
    active = jax.nn.silu(first).astype(BF16)
    inner = jnp.dot(active, inner_weight, preferred_element_type=F32)
    second = jax.nn.silu(inner).astype(BF16)
    hidden = first + jnp.dot(second, outer_weight, preferred_element_type=F32)
    third = jax.nn.silu(hidden).astype(BF16)
    predicted = jnp.dot(third, final_weight, preferred_element_type=F32)
    differ = predicted - target
    return 0.5 * jnp.sum(weight_mask * differ * differ)


def head_grads(first, inner_weight, outer_weight, final_weight, target, weight_mask):

    def head_loss(first_in, inner_in, outer_in, final_in):
        return tail(first_in, target, weight_mask, inner_in, outer_in, final_in)

    loss_value, pullback = jax.vjp(head_loss, first, inner_weight, outer_weight, final_weight)
    return pullback(jnp.ones((), F32))


def on_device(
    tokens,
    obs_mask,
    norm_gains,
    attn_in,
    attn_out,
    mlp_in,
    mlp_out,
    embodiment,
    levels,
    actions,
    noise,
    action_dims,
    head_read,
    head_act,
    time_table,
    block_in,
    block_out,
    head_out,
):
    width = attn_in.shape[3]
    heads = width // HDIM
    peers = lax.axis_size(DP)
    my_model = lax.axis_index("mp")
    my_owner = lax.axis_index(DP)

    full = jnp.concatenate(
        [
            jnp.moveaxis(attn_in[1], 0, 1).reshape(12, -1),
            attn_out[1].T,
            mlp_in[0],
            mlp_out[0].T,
        ],
        axis=1,
    )
    groups = full.shape[1] // width
    full = sent_to_all(full, "mp").reshape(2, 2, 12, groups, width)
    full = full.transpose(0, 2, 3, 1, 4).reshape(2, 12, -1)
    share = jnp.stack([mlp_in[1], mlp_out[1].T], axis=1).reshape(12, 2, 2, -1)
    share = share.transpose(2, 0, 1, 3).reshape(2, 12, -1)
    halves = jnp.concatenate([full, share], axis=2)
    halves = lax.all_to_all(halves, "c", split_axis=0, concat_axis=0, tiled=True)
    piece = halves.reshape(24, -1)

    owners = embodiment[:, 0]
    place = (jnp.arange(peers)[:, None] == owners[None, :]).astype(BF16)
    noisy = noisy_pair(levels, actions, noise, plan())
    marks = (levels + 1).astype(BF16)[..., None]
    early = jnp.concatenate([noisy, noise, marks, jnp.zeros((*levels.shape, 15), BF16)], axis=-1)
    sent = jnp.einsum("es,srf->erf", place, early, preferred_element_type=F32).astype(BF16)
    residual = tokens.astype(F32)
    normed = normalize(residual, norm_gains[0]).astype(BF16)
    mask_row = jnp.pad(obs_mask.reshape(1, -1).astype(BF16), ((0, 15), (0, D - obs_mask.size)))
    rows = jnp.concatenate([normed, mask_row], axis=0)
    first_piece = jnp.concatenate(
        [jnp.moveaxis(attn_in[0], 0, 1).reshape(12, -1), attn_out[0].T], axis=1
    )
    piece, rows = lax.optimization_barrier((piece, rows))
    gathered_weights = lax.all_gather(piece, ("c", "z", "y"), axis=0, tiled=True)

    for axis, step in (("z", 1), ("z", 2), ("z", 4), ("y", 1), ("y", 2), ("c", 1)):
        swapped = [(k, k ^ step) for k in range(lax.axis_size(axis))]
        other = lax.ppermute(first_piece, axis, swapped)
        upper = (lax.axis_index(axis) // step) % 2 == 1
        low = jnp.where(upper, other, first_piece)
        high = jnp.where(upper, first_piece, other)
        first_piece = jnp.concatenate([low, high], axis=0)
    first_weight = first_piece.reshape(2, 4, 8, 12, -1).transpose(2, 1, 0, 3, 4).reshape(D, -1)
    arrived = sent_to_all(rows, "mp")
    own_rows = normed.shape[0]
    gathered = arrived[:, :own_rows].reshape(-1, D)
    mask_group = arrived[:, own_rows, :own_rows].astype(jnp.int32).reshape(-1, SEQ)
    samples = mask_group.shape[0]
    projected = mm(gathered, first_weight[:, : 3 * width]).astype(BF16)
    projected = jnp.moveaxis(projected.reshape(-1, 3, width), 1, 0)
    projected = projected.reshape(3, samples, SEQ, heads, HDIM)
    context = attend(projected[0], projected[1], projected[2], allowed_keys(mask_group))
    partial_value = mm_t(context.reshape(-1, width), first_weight[:, 3 * width :])
    partial_value, sent = lax.optimization_barrier((partial_value.astype(BF16), sent))
    residual = residual + summed_on_arrival(partial_value, "mp")
    got = lax.all_to_all(sent, DP, split_axis=0, concat_axis=0, tiled=True)
    got = got.reshape(peers * READ, 128)

    residual, got, gathered_weights = lax.optimization_barrier((residual, got, gathered_weights))
    ending = trunk_rows(residual, obs_mask.reshape(1, -1), norm_gains, gathered_weights)
    ending = gather_rows(ending[: 2 * obs_mask.shape[0]], "mp")
    partial_value = readout_mlp(ending, norm_gains, gathered_weights)
    ending = ending.astype(F32) + summed_for_all(partial_value, "mp")
    readouts = normalize(ending, norm_gains[4]).astype(BF16).reshape(samples, READ * D)

    send = mm(place, readouts).astype(BF16)
    features = lax.all_to_all(send, DP, split_axis=0, concat_axis=0, tiled=True)
    features = features.reshape(peers * READ, D)
    head_noisy = got[:, :ACT]
    head_target = got[:, ACT : 2 * ACT].astype(F32)
    head_level = got[:, 2 * ACT].astype(jnp.int32) - 1
    onehot = (head_level[:, None] == jnp.arange(LEVELS)).astype(BF16)
    dims_here = jnp.sum(jnp.where(jnp.arange(EMB) == my_owner, action_dims, 0))
    column = jnp.arange(ACT) % ADIM_MAX
    weight_mask = (head_level >= 0).astype(F32)[:, None] * (column < dims_here).astype(F32)[None, :]
    others = mm(head_noisy, head_act[0]) + mm(onehot, time_table[0])
    first = mm(features, head_read[0]) + others
    grad_first, grad_inner, grad_outer, grad_final = head_grads(
        first,
        block_in[0].astype(F32),
        block_out[0].astype(F32),
        head_out[0].astype(F32),
        head_target,
        weight_mask,
    )
    grad_bf = grad_first.astype(BF16)
    backward = jnp.einsum("nc,dc->nd", grad_bf, head_read[0], preferred_element_type=F32)
    backward = backward.astype(BF16).reshape(peers, READ * D)
    arrived = lax.all_to_all(backward, DP, split_axis=0, concat_axis=0, tiled=True)
    mine = samples // 4
    own_place = lax.dynamic_slice_in_dim(place, my_model * mine, mine, 1)
    arrived = jnp.einsum("es,ef->sf", own_place, arrived, preferred_element_type=F32)
    arrived = arrived.astype(BF16).reshape(mine, READ, D)
    part = lax.dynamic_slice_in_dim(features, my_model * width, width, 1)
    grad_read = jnp.einsum("nd,nc->dc", part, grad_bf, preferred_element_type=F32)
    grad_act = jnp.einsum("na,nc->ac", head_noisy, grad_bf, preferred_element_type=F32)
    grad_time = jnp.einsum("nl,nc->lc", onehot, grad_bf, preferred_element_type=F32)
    return (
        arrived,
        grad_read[None],
        grad_act[None],
        grad_time[None],
        grad_inner[None],
        grad_outer[None],
        grad_final[None],
    )


def solution(mesh):
    fine = Mesh(mesh.devices.reshape(8, 4, 2, 4), ("z", "y", "c", "mp"))
    both = (*DP, "mp")
    placed = (
        P(both, None),
        P(both, None),
        P(),
        P(None, None, DP, "mp"),
        P(None, "mp", DP),
        P(None, DP, "mp"),
        P(None, "mp", DP),
        P(DP, None),
        P(DP, None),
        P(DP, None, None),
        P(DP, None, None),
        P(),
        P(DP, None, None),
        P(DP, None, None),
        P(DP, None, None),
        P(DP, None, None),
        P(DP, None, None),
        P(DP, None, None),
    )
    return jax.shard_map(
        on_device,
        mesh=fine,
        in_specs=placed,
        out_specs=(
            P(both, None, None),
            P(DP, "mp", None),
            P(DP, None, None),
            P(DP, None, None),
            P(DP, None, None),
            P(DP, None, None),
            P(DP, None, None),
        ),
        check_vma=False,
    )
```

```python
import math

import jax
import jax.numpy as jnp
from jax import lax
from jax.experimental import pallas as pl
from jax.experimental.pallas import tpu as pltpu
from jax.sharding import Mesh, PartitionSpec as P

D = 768
HDIM = 64
EMB = 25
READ = 2
LEVELS = 20
ADIM_MAX = 14
ACT = 56
SEQ = 64
F32 = jnp.float32
BF16 = jnp.bfloat16
DP = ("z", "y", "c")


norm_eps = 1e-05


def sent_to_all(x, axis):
    copies = jnp.broadcast_to(x, (lax.axis_size(axis), *x.shape))
    return lax.all_to_all(copies, axis, split_axis=0, concat_axis=0, tiled=True)


def summed_on_arrival(x, axis):
    pieces = x.reshape(lax.axis_size(axis), -1, x.shape[1])
    arrived = lax.all_to_all(pieces, axis, split_axis=0, concat_axis=0, tiled=True)
    return arrived.astype(F32).sum(axis=0)


def normalize(values, scale_gain):
    center = values - jnp.mean(values, axis=-1, keepdims=True)
    spread = jnp.mean(center * center, axis=-1, keepdims=True)
    return center * lax.rsqrt(spread + norm_eps) * scale_gain


def mm(a, b):
    return jnp.dot(a, b, preferred_element_type=F32)


def mm_t(a, b):
    return jnp.einsum("tk,dk->td", a, b, preferred_element_type=F32)


def allowed_keys(observed):
    length = observed.shape[1]
    position = jnp.arange(length)
    visible = (observed == 1) & (position < length - READ)[None, :]
    itself = position[:, None] == position[None, :]
    return visible[:, None, :] | itself[None, :, :]


def attend(queries, key_rows, value_rows, allowed):
    scores = jnp.einsum(
        "sqhd,skhd->shqk", queries, key_rows, preferred_element_type=F32
    ) * HDIM ** (-0.5)
    weights = jnp.where(allowed[:, None, :, :], jnp.exp(scores), 0.0)
    shares = (weights / jnp.sum(weights, axis=-1, keepdims=True)).astype(BF16)
    context = jnp.einsum("shqk,skhd->sqhd", shares, value_rows, preferred_element_type=F32)
    return context.astype(BF16)


def nt(a, b):
    return lax.dot_general(a, b, (((1,), (1,)), ((), ())), preferred_element_type=F32)


def trunk_rows_kernel(res_ref, mask_ref, gain_ref, all_ref, out_ref, mlp, att, mlp_sem, att_sem):
    def block(side, part):
        return pltpu.make_async_copy(
            all_ref.at[pl.ds(side * D, D), pl.ds(1536 * (part + 1), 1536)],
            mlp.at[side, part],
            mlp_sem.at[side, part],
        )

    def attention(side):
        return pltpu.make_async_copy(
            all_ref.at[pl.ds(side * D, D), pl.ds(0, 1536)], att.at[side], att_sem.at[side]
        )

    for side in range(2):
        for part in range(2):
            block(side, part).start()
    for side in range(2):
        attention(side).start()
    residual = res_ref[...]
    normed = normalize(residual, gain_ref[1:2, :]).astype(BF16)
    for side in range(2):
        block(side, 0).wait()
        hidden = jax.nn.gelu(mm(normed, mlp[side, 0]), approximate=True).astype(BF16)
        block(side, 1).wait()
        residual = residual + nt(hidden, mlp[side, 1])
    normed = normalize(residual, gain_ref[2:3, :])
    ends = [residual[SEQ * k + SEQ - READ : SEQ * (k + 1)] for k in (0, 1, 2, 2)]
    ending = jnp.concatenate(ends, axis=0)
    ends = [normed[SEQ * k + SEQ - READ : SEQ * (k + 1)] for k in (0, 1, 2, 2)]
    normed_end = jnp.concatenate(ends, axis=0).astype(BF16)
    normed = normed.astype(BF16)
    rows, keys, width = 48, residual.shape[0], 384
    row = lax.broadcasted_iota(jnp.int32, (rows, keys), 0) % 8
    key = lax.broadcasted_iota(jnp.int32, (rows, keys), 1)
    place = key % SEQ
    seen = (mask_ref[...] == 1) & (place < SEQ - READ)
    allowed = (key // SEQ == jnp.minimum(row // READ, 2)) & (
        seen | (place == SEQ - READ + row % READ)
    )
    own_head = (
        lax.broadcasted_iota(jnp.int32, (rows, width), 0) // 8
        == lax.broadcasted_iota(jnp.int32, (rows, width), 1) // HDIM
    )
    for side in range(2):
        attention(side).wait()
        queries = mm(normed_end, att[side, :, 0:384]).astype(BF16).astype(F32)
        key_rows = mm(normed, att[side, :, 384:768]).astype(BF16)
        value_rows = mm(normed, att[side, :, 768:1152]).astype(BF16)
        spread = jnp.where(own_head, jnp.concatenate([queries] * 6, axis=0), 0.0).astype(BF16)
        scores = nt(spread, key_rows) * HDIM ** (-0.5)
        weights = jnp.where(allowed, jnp.exp(scores), 0.0)
        shares = (weights / jnp.sum(weights, axis=-1, keepdims=True)).astype(BF16)
        context = jnp.where(own_head, mm(shares, value_rows), 0.0)
        context = sum(context[8 * k : 8 * k + 8] for k in range(6)).astype(BF16)
        ending = ending + nt(context, att[side, :, 1152:1536])
    for member in range(4):
        out_ref[member] = ending.astype(BF16)


def trunk_rows(residual, mask_row, gains, weights):
    vmem = pl.BlockSpec(memory_space=pltpu.VMEM)
    rows = (residual, mask_row, gains)
    return pl.pallas_call(
        trunk_rows_kernel,
        out_shape=jax.ShapeDtypeStruct((4, 8, D), BF16),
        in_specs=[vmem, vmem, vmem, pl.BlockSpec(memory_space=pl.ANY)],
        out_specs=vmem,
        scratch_shapes=[
            pltpu.VMEM((2, 2, D, 1536), BF16),
            pltpu.VMEM((2, D, 1536), BF16),
            pltpu.SemaphoreType.DMA((2, 2)),
            pltpu.SemaphoreType.DMA((2,)),
        ],
        compiler_params=pltpu.CompilerParams(vmem_limit_bytes=40 * 1024 * 1024),
        name="trunk_rows",
    )(*(pltpu.with_memory_space_constraint(a, pltpu.VMEM) for a in rows), weights)


def readout_mlp_kernel(end_ref, gain_ref, first_ref, second_ref, out_ref):
    normed = normalize(end_ref[...].astype(F32), gain_ref[3:4, :]).astype(BF16)
    total = jnp.zeros(end_ref.shape, F32)
    for side_ref in (first_ref, second_ref):
        hidden = jax.nn.gelu(mm(normed, side_ref[:, 0:384]), approximate=True).astype(BF16)
        total = total + nt(hidden, side_ref[:, 384:768])
    for member in range(4):
        out_ref[member] = total.astype(BF16)


def readout_mlp(ending, gains, first_side, second_side):
    vmem = pl.BlockSpec(memory_space=pltpu.VMEM)
    operands = (ending, gains, first_side, second_side)
    return pl.pallas_call(
        readout_mlp_kernel,
        out_shape=jax.ShapeDtypeStruct((4, *ending.shape), BF16),
        in_specs=[vmem] * 4,
        out_specs=vmem,
        name="readout_mlp",
    )(*(pltpu.with_memory_space_constraint(a, pltpu.VMEM) for a in operands))


def plan():
    steps_up = (jnp.arange(LEVELS, dtype=F32) + 1.0) / LEVELS
    anchor = math.cos(0.008 / 1.008 * math.pi / 2) ** 2
    return jnp.cos((steps_up + 0.008) / 1.008 * (math.pi / 2)) ** 2 / anchor


def noisy_pair(level_ids, clean, noise_draw, table):
    picked = (level_ids[..., None] == jnp.arange(LEVELS)).astype(F32)
    kept = jnp.sum(picked * table, axis=-1)[..., None]
    mixed = jnp.sqrt(kept) * clean.astype(F32) + jnp.sqrt(1.0 - kept) * noise_draw.astype(F32)
    return mixed.astype(BF16)


def tail(first, target, weight_mask, inner_weight, outer_weight, final_weight):
    active = jax.nn.silu(first).astype(BF16)
    inner = jnp.dot(active, inner_weight, preferred_element_type=F32)
    second = jax.nn.silu(inner).astype(BF16)
    hidden = first + jnp.dot(second, outer_weight, preferred_element_type=F32)
    third = jax.nn.silu(hidden).astype(BF16)
    predicted = jnp.dot(third, final_weight, preferred_element_type=F32)
    differ = predicted - target
    return 0.5 * jnp.sum(weight_mask * differ * differ)


def head_grads(first, inner_weight, outer_weight, final_weight, target, weight_mask):

    def head_loss(first_in, inner_in, outer_in, final_in):
        return tail(first_in, target, weight_mask, inner_in, outer_in, final_in)

    loss_value, pullback = jax.vjp(head_loss, first, inner_weight, outer_weight, final_weight)
    return pullback(jnp.ones((), F32))


def on_device(
    tokens,
    obs_mask,
    norm_gains,
    attn_in,
    attn_out,
    mlp_in,
    mlp_out,
    embodiment,
    levels,
    actions,
    noise,
    action_dims,
    head_read,
    head_act,
    time_table,
    block_in,
    block_out,
    head_out,
):
    width = attn_in.shape[3]
    heads = width // HDIM
    peers = lax.axis_size(DP)
    my_model = lax.axis_index("mp")
    my_owner = lax.axis_index(DP)

    full = jnp.concatenate(
        [
            jnp.moveaxis(attn_in[1], 0, 1).reshape(12, -1),
            attn_out[1].T,
            mlp_in[0],
            mlp_out[0].T,
        ],
        axis=1,
    )
    groups = full.shape[1] // width
    full = sent_to_all(full, "mp").reshape(2, 2, 12, groups, width)
    full = full.transpose(0, 2, 3, 1, 4).reshape(2, 12, -1)
    share = jnp.stack([mlp_in[1], mlp_out[1].T], axis=1).reshape(12, 2, 2, -1)
    share = share.transpose(2, 0, 1, 3).reshape(2, 12, -1)
    halves = jnp.concatenate([full, share], axis=2)
    upper = lax.axis_index("c") == 1
    mine = jnp.where(upper, halves[1], halves[0])
    other = lax.ppermute(jnp.where(upper, halves[0], halves[1]), "c", [(0, 1), (1, 0)])
    piece = jnp.concatenate(
        [jnp.where(upper, other, mine), jnp.where(upper, mine, other)], axis=0
    )

    owners = embodiment[:, 0]
    place = (jnp.arange(peers)[:, None] == owners[None, :]).astype(BF16)
    row_owner = jnp.pad(owners.reshape(4, 3), ((0, 0), (0, 1)), constant_values=-1)
    row_owner = jnp.repeat(row_owner.reshape(-1), READ)
    target = jnp.arange(peers * READ)
    row_place = (target[:, None] // READ == row_owner[None, :]) & (
        target[:, None] % READ == jnp.arange(row_owner.size)[None, :] % READ
    )
    row_place = row_place.astype(BF16)
    noisy = noisy_pair(levels, actions, noise, plan())
    marks = (levels + 1).astype(BF16)[..., None]
    early = jnp.concatenate([noisy, noise, marks, jnp.zeros((*levels.shape, 15), BF16)], axis=-1)
    sent = jnp.einsum("es,srf->erf", place, early, preferred_element_type=F32).astype(BF16)
    residual = tokens.astype(F32)
    normed = normalize(residual, norm_gains[0]).astype(BF16)
    mask_row = jnp.pad(obs_mask.reshape(1, -1).astype(BF16), ((0, 15), (0, D - obs_mask.size)))
    rows = jnp.concatenate([normed, mask_row], axis=0)
    first_piece = jnp.concatenate(
        [jnp.moveaxis(attn_in[0], 0, 1).reshape(12, -1), attn_out[0].T], axis=1
    )
    piece, rows = lax.optimization_barrier((piece, rows))
    gathered_weights = lax.all_gather(piece, ("c", "z", "y"), axis=0, tiled=True)

    for axis, step in (("z", 1), ("z", 2), ("z", 4), ("y", 1), ("y", 2), ("c", 1)):
        swapped = [(k, k ^ step) for k in range(lax.axis_size(axis))]
        other = lax.ppermute(first_piece, axis, swapped)
        upper = (lax.axis_index(axis) // step) % 2 == 1
        low = jnp.where(upper, other, first_piece)
        high = jnp.where(upper, first_piece, other)
        first_piece = jnp.concatenate([low, high], axis=0)
    first_weight = first_piece.reshape(2, 4, 8, 12, -1).transpose(2, 1, 0, 3, 4).reshape(D, -1)
    arrived = sent_to_all(rows, "mp")
    own_rows = normed.shape[0]
    gathered = arrived[:, :own_rows].reshape(-1, D)
    mask_group = arrived[:, own_rows, :own_rows].astype(jnp.int32).reshape(-1, SEQ)
    samples = mask_group.shape[0]
    projected = mm(gathered, first_weight[:, : 3 * width]).astype(BF16)
    projected = jnp.moveaxis(projected.reshape(-1, 3, width), 1, 0)
    projected = projected.reshape(3, samples, SEQ, heads, HDIM)
    context = attend(projected[0], projected[1], projected[2], allowed_keys(mask_group))
    partial_value = mm_t(context.reshape(-1, width), first_weight[:, 3 * width :])
    partial_value, sent = lax.optimization_barrier((partial_value.astype(BF16), sent))
    residual = residual + summed_on_arrival(partial_value, "mp")
    got = lax.all_to_all(sent, DP, split_axis=0, concat_axis=0, tiled=True)
    got = got.reshape(peers * READ, 128)

    residual, got, gathered_weights = lax.optimization_barrier((residual, got, gathered_weights))
    sides = [gathered_weights[D * k : D * (k + 1), 4608:5376] for k in range(2)]
    copies = trunk_rows(residual, obs_mask.reshape(1, -1), norm_gains, gathered_weights)
    ending = lax.all_to_all(copies, "mp", split_axis=0, concat_axis=0, tiled=True)
    ending = ending.reshape(-1, D)
    copies = readout_mlp(ending, norm_gains, *sides)
    terms = lax.all_to_all(copies, "mp", split_axis=0, concat_axis=0, tiled=True)
    ending = ending.astype(F32) + terms.astype(F32).sum(axis=0)
    readouts = normalize(ending, norm_gains[4]).astype(BF16)

    send = mm(row_place, readouts).astype(BF16).reshape(peers, READ, D)
    features = lax.all_to_all(send, DP, split_axis=0, concat_axis=0, tiled=True)
    features = features.reshape(peers * READ, D)
    head_noisy = got[:, :ACT]
    head_target = got[:, ACT : 2 * ACT].astype(F32)
    head_level = got[:, 2 * ACT].astype(jnp.int32) - 1
    onehot = (head_level[:, None] == jnp.arange(LEVELS)).astype(BF16)
    dims_here = jnp.sum(jnp.where(jnp.arange(EMB) == my_owner, action_dims, 0))
    column = jnp.arange(ACT) % ADIM_MAX
    weight_mask = (head_level >= 0).astype(F32)[:, None] * (column < dims_here).astype(F32)[None, :]
    others = mm(head_noisy, head_act[0]) + mm(onehot, time_table[0])
    first = mm(features, head_read[0]) + others
    grad_first, grad_inner, grad_outer, grad_final = head_grads(
        first,
        block_in[0].astype(F32),
        block_out[0].astype(F32),
        head_out[0].astype(F32),
        head_target,
        weight_mask,
    )
    grad_bf = grad_first.astype(BF16)
    backward = jnp.einsum("nc,dc->nd", grad_bf, head_read[0], preferred_element_type=F32)
    backward = backward.astype(BF16).reshape(peers, READ, D)
    backward, features = lax.optimization_barrier((backward, features))
    arrived = lax.all_to_all(backward, DP, split_axis=0, concat_axis=0, tiled=True)
    mine = samples // 4
    own_place = lax.dynamic_slice_in_dim(place, my_model * mine, mine, 1)
    arrived = jnp.einsum("es,erf->srf", own_place, arrived, preferred_element_type=F32)
    arrived = arrived.astype(BF16)
    part = lax.dynamic_slice_in_dim(features, my_model * width, width, 1)
    grad_read = jnp.einsum("nd,nc->dc", part, grad_bf, preferred_element_type=F32)
    grad_act = jnp.einsum("na,nc->ac", head_noisy, grad_bf, preferred_element_type=F32)
    grad_time = jnp.einsum("nl,nc->lc", onehot, grad_bf, preferred_element_type=F32)
    return (
        arrived,
        grad_read[None],
        grad_act[None],
        grad_time[None],
        grad_inner[None],
        grad_outer[None],
        grad_final[None],
    )


def solution(mesh):
    fine = Mesh(mesh.devices.reshape(8, 4, 2, 4), ("z", "y", "c", "mp"))
    both = (*DP, "mp")
    placed = (
        P(both, None),
        P(both, None),
        P(),
        P(None, None, DP, "mp"),
        P(None, "mp", DP),
        P(None, DP, "mp"),
        P(None, "mp", DP),
        P(DP, None),
        P(DP, None),
        P(DP, None, None),
        P(DP, None, None),
        P(),
        P(DP, None, None),
        P(DP, None, None),
        P(DP, None, None),
        P(DP, None, None),
        P(DP, None, None),
        P(DP, None, None),
    )
    return jax.shard_map(
        on_device,
        mesh=fine,
        in_specs=placed,
        out_specs=(
            P(both, None, None),
            P(DP, "mp", None),
            P(DP, None, None),
            P(DP, None, None),
            P(DP, None, None),
            P(DP, None, None),
            P(DP, None, None),
        ),
        check_vma=False,
    )
```

```python
import math

import jax
import jax.numpy as jnp
from jax import lax
from jax.experimental import pallas as pl
from jax.experimental.pallas import tpu as pltpu
from jax.sharding import Mesh, PartitionSpec as P

D = 768
HDIM = 64
EMB = 25
READ = 2
LEVELS = 20
ADIM_MAX = 14
ACT = 56
SEQ = 64
F32 = jnp.float32
BF16 = jnp.bfloat16
DP = ("z", "y", "c")


norm_eps = 1e-05


def sent_to_all(x, axis):
    copies = jnp.broadcast_to(x, (lax.axis_size(axis), *x.shape))
    return lax.all_to_all(copies, axis, split_axis=0, concat_axis=0, tiled=True)


def summed_on_arrival(x, axis):
    pieces = x.reshape(lax.axis_size(axis), -1, x.shape[1])
    arrived = lax.all_to_all(pieces, axis, split_axis=0, concat_axis=0, tiled=True)
    return arrived.astype(F32).sum(axis=0)


def normalize(values, scale_gain):
    center = values - jnp.mean(values, axis=-1, keepdims=True)
    spread = jnp.mean(center * center, axis=-1, keepdims=True)
    return center * lax.rsqrt(spread + norm_eps) * scale_gain


def mm(a, b):
    return jnp.dot(a, b, preferred_element_type=F32)


def mm_t(a, b):
    return jnp.einsum("tk,dk->td", a, b, preferred_element_type=F32)


def allowed_keys(observed):
    length = observed.shape[1]
    position = jnp.arange(length)
    visible = (observed == 1) & (position < length - READ)[None, :]
    itself = position[:, None] == position[None, :]
    return visible[:, None, :] | itself[None, :, :]


def attend(queries, key_rows, value_rows, allowed):
    scores = jnp.einsum(
        "sqhd,skhd->shqk", queries, key_rows, preferred_element_type=F32
    ) * HDIM ** (-0.5)
    weights = jnp.where(allowed[:, None, :, :], jnp.exp(scores), 0.0)
    shares = (weights / jnp.sum(weights, axis=-1, keepdims=True)).astype(BF16)
    context = jnp.einsum("shqk,skhd->sqhd", shares, value_rows, preferred_element_type=F32)
    return context.astype(BF16)


def nt(a, b):
    return lax.dot_general(a, b, (((1,), (1,)), ((), ())), preferred_element_type=F32)


def trunk_rows_kernel(res_ref, mask_ref, gain_ref, all_ref, out_ref, mlp, att, mlp_sem, att_sem):
    def block(side, part):
        return pltpu.make_async_copy(
            all_ref.at[pl.ds(side * D, D), pl.ds(1536 * (part + 1), 1536)],
            mlp.at[side, part],
            mlp_sem.at[side, part],
        )

    def attention(side):
        return pltpu.make_async_copy(
            all_ref.at[pl.ds(side * D, D), pl.ds(0, 1536)], att.at[side], att_sem.at[side]
        )

    for side in range(2):
        for part in range(2):
            block(side, part).start()
    for side in range(2):
        attention(side).start()
    residual = res_ref[...]
    normed = normalize(residual, gain_ref[1:2, :]).astype(BF16)
    for side in range(2):
        block(side, 0).wait()
        hidden = jax.nn.gelu(mm(normed, mlp[side, 0]), approximate=True).astype(BF16)
        block(side, 1).wait()
        residual = residual + nt(hidden, mlp[side, 1])
    normed = normalize(residual, gain_ref[2:3, :])
    ends = [residual[SEQ * k + SEQ - READ : SEQ * (k + 1)] for k in (0, 1, 2, 2)]
    ending = jnp.concatenate(ends, axis=0)
    ends = [normed[SEQ * k + SEQ - READ : SEQ * (k + 1)] for k in (0, 1, 2, 2)]
    normed_end = jnp.concatenate(ends, axis=0).astype(BF16)
    normed = normed.astype(BF16)
    rows, keys, width = 48, residual.shape[0], 384
    row = lax.broadcasted_iota(jnp.int32, (rows, keys), 0) % 8
    key = lax.broadcasted_iota(jnp.int32, (rows, keys), 1)
    place = key % SEQ
    seen = (mask_ref[...] == 1) & (place < SEQ - READ)
    allowed = (key // SEQ == jnp.minimum(row // READ, 2)) & (
        seen | (place == SEQ - READ + row % READ)
    )
    own_head = (
        lax.broadcasted_iota(jnp.int32, (rows, width), 0) // 8
        == lax.broadcasted_iota(jnp.int32, (rows, width), 1) // HDIM
    )
    for side in range(2):
        attention(side).wait()
        queries = mm(normed_end, att[side, :, 0:384]).astype(BF16).astype(F32)
        key_rows = mm(normed, att[side, :, 384:768]).astype(BF16)
        value_rows = mm(normed, att[side, :, 768:1152]).astype(BF16)
        spread = jnp.where(own_head, jnp.concatenate([queries] * 6, axis=0), 0.0).astype(BF16)
        scores = nt(spread, key_rows) * HDIM ** (-0.5)
        weights = jnp.where(allowed, jnp.exp(scores), 0.0)
        shares = (weights / jnp.sum(weights, axis=-1, keepdims=True)).astype(BF16)
        context = jnp.where(own_head, mm(shares, value_rows), 0.0)
        context = sum(context[8 * k : 8 * k + 8] for k in range(6)).astype(BF16)
        ending = ending + nt(context, att[side, :, 1152:1536])
    for member in range(4):
        out_ref[member] = ending.astype(BF16)


def trunk_rows(residual, mask_row, gains, weights):
    vmem = pl.BlockSpec(memory_space=pltpu.VMEM)
    rows = (residual, mask_row, gains)
    return pl.pallas_call(
        trunk_rows_kernel,
        out_shape=jax.ShapeDtypeStruct((4, 8, D), BF16),
        in_specs=[vmem, vmem, vmem, pl.BlockSpec(memory_space=pl.ANY)],
        out_specs=vmem,
        scratch_shapes=[
            pltpu.VMEM((2, 2, D, 1536), BF16),
            pltpu.VMEM((2, D, 1536), BF16),
            pltpu.SemaphoreType.DMA((2, 2)),
            pltpu.SemaphoreType.DMA((2,)),
        ],
        compiler_params=pltpu.CompilerParams(vmem_limit_bytes=40 * 1024 * 1024),
        name="trunk_rows",
    )(*(pltpu.with_memory_space_constraint(a, pltpu.VMEM) for a in rows), weights)


def readout_mlp_kernel(end_ref, gain_ref, first_ref, second_ref, out_ref):
    normed = normalize(end_ref[...].astype(F32), gain_ref[3:4, :]).astype(BF16)
    total = jnp.zeros(end_ref.shape, F32)
    for side_ref in (first_ref, second_ref):
        hidden = jax.nn.gelu(mm(normed, side_ref[:, 0:384]), approximate=True).astype(BF16)
        total = total + nt(hidden, side_ref[:, 384:768])
    for member in range(4):
        out_ref[member] = total.astype(BF16)


def readout_mlp(ending, gains, first_side, second_side):
    vmem = pl.BlockSpec(memory_space=pltpu.VMEM)
    operands = (ending, gains, first_side, second_side)
    return pl.pallas_call(
        readout_mlp_kernel,
        out_shape=jax.ShapeDtypeStruct((4, *ending.shape), BF16),
        in_specs=[vmem] * 4,
        out_specs=vmem,
        name="readout_mlp",
    )(*(pltpu.with_memory_space_constraint(a, pltpu.VMEM) for a in operands))


def plan():
    steps_up = (jnp.arange(LEVELS, dtype=F32) + 1.0) / LEVELS
    anchor = math.cos(0.008 / 1.008 * math.pi / 2) ** 2
    return jnp.cos((steps_up + 0.008) / 1.008 * (math.pi / 2)) ** 2 / anchor


def noisy_pair(level_ids, clean, noise_draw, table):
    picked = (level_ids[..., None] == jnp.arange(LEVELS)).astype(F32)
    kept = jnp.sum(picked * table, axis=-1)[..., None]
    mixed = jnp.sqrt(kept) * clean.astype(F32) + jnp.sqrt(1.0 - kept) * noise_draw.astype(F32)
    return mixed.astype(BF16)


def tail(first, target, weight_mask, inner_weight, outer_weight, final_weight):
    active = jax.nn.silu(first).astype(BF16)
    inner = jnp.dot(active, inner_weight, preferred_element_type=F32)
    second = jax.nn.silu(inner).astype(BF16)
    hidden = first + jnp.dot(second, outer_weight, preferred_element_type=F32)
    third = jax.nn.silu(hidden).astype(BF16)
    predicted = jnp.dot(third, final_weight, preferred_element_type=F32)
    differ = predicted - target
    return 0.5 * jnp.sum(weight_mask * differ * differ)


def head_grads(first, inner_weight, outer_weight, final_weight, target, weight_mask):

    def head_loss(first_in, inner_in, outer_in, final_in):
        return tail(first_in, target, weight_mask, inner_in, outer_in, final_in)

    loss_value, pullback = jax.vjp(head_loss, first, inner_weight, outer_weight, final_weight)
    return pullback(jnp.ones((), F32))


def on_device(
    tokens,
    obs_mask,
    norm_gains,
    attn_in,
    attn_out,
    mlp_in,
    mlp_out,
    embodiment,
    levels,
    actions,
    noise,
    action_dims,
    head_read,
    head_act,
    time_table,
    block_in,
    block_out,
    head_out,
):
    width = attn_in.shape[3]
    heads = width // HDIM
    peers = lax.axis_size(DP)
    my_model = lax.axis_index("mp")
    my_owner = lax.axis_index(DP)

    full = jnp.concatenate(
        [
            jnp.moveaxis(attn_in[1], 0, 1).reshape(12, -1),
            attn_out[1].T,
            mlp_in[0],
            mlp_out[0].T,
        ],
        axis=1,
    )
    groups = full.shape[1] // width
    full = sent_to_all(full, "mp").reshape(2, 2, 12, groups, width)
    full = full.transpose(0, 2, 3, 1, 4).reshape(2, 12, -1)
    share = jnp.stack([mlp_in[1], mlp_out[1].T], axis=1).reshape(12, 2, 2, -1)
    share = share.transpose(2, 0, 1, 3).reshape(2, 12, -1)
    halves = jnp.concatenate([full, share], axis=2)
    upper = lax.axis_index("c") == 1
    mine = jnp.where(upper, halves[1], halves[0])
    other = lax.ppermute(jnp.where(upper, halves[0], halves[1]), "c", [(0, 1), (1, 0)])
    piece = jnp.concatenate(
        [jnp.where(upper, other, mine), jnp.where(upper, mine, other)], axis=0
    )

    owners = embodiment[:, 0]
    place = (jnp.arange(peers)[:, None] == owners[None, :]).astype(BF16)
    row_owner = jnp.pad(owners.reshape(4, 3), ((0, 0), (0, 1)), constant_values=-1)
    row_owner = jnp.repeat(row_owner.reshape(-1), READ)
    target = jnp.arange(peers * READ)
    row_place = (target[:, None] // READ == row_owner[None, :]) & (
        target[:, None] % READ == jnp.arange(row_owner.size)[None, :] % READ
    )
    row_place = row_place.astype(BF16)
    noisy = noisy_pair(levels, actions, noise, plan())
    marks = (levels + 1).astype(BF16)[..., None]
    early = jnp.concatenate([noisy, noise, marks, jnp.zeros((*levels.shape, 15), BF16)], axis=-1)
    sent = jnp.einsum("es,srf->erf", place, early, preferred_element_type=F32).astype(BF16)
    residual = tokens.astype(F32)
    normed = normalize(residual, norm_gains[0]).astype(BF16)
    mask_row = jnp.pad(obs_mask.reshape(1, -1).astype(BF16), ((0, 15), (0, D - obs_mask.size)))
    rows = jnp.concatenate([normed, mask_row], axis=0)
    first_piece = jnp.concatenate(
        [jnp.moveaxis(attn_in[0], 0, 1).reshape(12, -1), attn_out[0].T], axis=1
    )
    piece, rows = lax.optimization_barrier((piece, rows))
    gathered_weights = lax.all_gather(piece, ("c", "z", "y"), axis=0, tiled=True)

    arrived = sent_to_all(rows, "mp")
    for axis, step in (("z", 1), ("z", 2), ("z", 4), ("y", 1), ("y", 2), ("c", 1)):
        if step == 2 and axis == "y":
            first_piece, arrived = lax.optimization_barrier((first_piece, arrived))
        swapped = [(k, k ^ step) for k in range(lax.axis_size(axis))]
        other = lax.ppermute(first_piece, axis, swapped)
        upper = (lax.axis_index(axis) // step) % 2 == 1
        low = jnp.where(upper, other, first_piece)
        high = jnp.where(upper, first_piece, other)
        first_piece = jnp.concatenate([low, high], axis=0)
    index = jnp.arange(D)
    owner = index // 12
    held = (owner % 2) * 32 + (owner // 2 % 4) * 8 + owner // 8
    order = (held * 12 + index % 12)[:, None] == index[None, :]
    first_weight = mm(order.astype(BF16), first_piece).astype(BF16)
    own_rows = normed.shape[0]
    gathered = arrived[:, :own_rows].reshape(-1, D)
    mask_group = arrived[:, own_rows, :own_rows].astype(jnp.int32).reshape(-1, SEQ)
    samples = mask_group.shape[0]
    projected = mm(gathered, first_weight[:, : 3 * width]).astype(BF16)
    projected = jnp.moveaxis(projected.reshape(-1, 3, width), 1, 0)
    projected = projected.reshape(3, samples, SEQ, heads, HDIM)
    context = attend(projected[0], projected[1], projected[2], allowed_keys(mask_group))
    partial_value = mm_t(context.reshape(-1, width), first_weight[:, 3 * width :])
    partial_value, sent = lax.optimization_barrier((partial_value.astype(BF16), sent))
    residual = residual + summed_on_arrival(partial_value, "mp")
    got = lax.all_to_all(sent, DP, split_axis=0, concat_axis=0, tiled=True)
    got = got.reshape(peers * READ, 128)

    residual, got, gathered_weights = lax.optimization_barrier((residual, got, gathered_weights))
    sides = [gathered_weights[D * k : D * (k + 1), 4608:5376] for k in range(2)]
    copies = trunk_rows(residual, obs_mask.reshape(1, -1), norm_gains, gathered_weights)
    ending = lax.all_to_all(copies, "mp", split_axis=0, concat_axis=0, tiled=True)
    ending = ending.reshape(-1, D)
    copies = readout_mlp(ending, norm_gains, *sides)
    terms = lax.all_to_all(copies, "mp", split_axis=0, concat_axis=0, tiled=True)
    ending = ending.astype(F32) + terms.astype(F32).sum(axis=0)
    readouts = normalize(ending, norm_gains[4]).astype(BF16)

    send = mm(row_place, readouts).astype(BF16).reshape(peers, READ, D)
    features = lax.all_to_all(send, DP, split_axis=0, concat_axis=0, tiled=True)
    features = features.reshape(peers * READ, D)
    head_noisy = got[:, :ACT]
    head_target = got[:, ACT : 2 * ACT].astype(F32)
    head_level = got[:, 2 * ACT].astype(jnp.int32) - 1
    onehot = (head_level[:, None] == jnp.arange(LEVELS)).astype(BF16)
    dims_here = jnp.sum(jnp.where(jnp.arange(EMB) == my_owner, action_dims, 0))
    column = jnp.arange(ACT) % ADIM_MAX
    weight_mask = (head_level >= 0).astype(F32)[:, None] * (column < dims_here).astype(F32)[None, :]
    others = mm(head_noisy, head_act[0]) + mm(onehot, time_table[0])
    first = mm(features, head_read[0]) + others
    grad_first, grad_inner, grad_outer, grad_final = head_grads(
        first,
        block_in[0].astype(F32),
        block_out[0].astype(F32),
        head_out[0].astype(F32),
        head_target,
        weight_mask,
    )
    grad_bf = grad_first.astype(BF16)
    backward = jnp.einsum("nc,dc->nd", grad_bf, head_read[0], preferred_element_type=F32)
    backward = backward.astype(BF16).reshape(peers, READ, D)
    backward, features = lax.optimization_barrier((backward, features))
    arrived = lax.all_to_all(backward, DP, split_axis=0, concat_axis=0, tiled=True)
    mine = samples // 4
    own_place = lax.dynamic_slice_in_dim(place, my_model * mine, mine, 1)
    arrived = jnp.einsum("es,erf->srf", own_place, arrived, preferred_element_type=F32)
    arrived = arrived.astype(BF16)
    part = lax.dynamic_slice_in_dim(features, my_model * width, width, 1)
    grad_read = jnp.einsum("nd,nc->dc", part, grad_bf, preferred_element_type=F32)
    grad_act = jnp.einsum("na,nc->ac", head_noisy, grad_bf, preferred_element_type=F32)
    grad_time = jnp.einsum("nl,nc->lc", onehot, grad_bf, preferred_element_type=F32)
    return (
        arrived,
        grad_read[None],
        grad_act[None],
        grad_time[None],
        grad_inner[None],
        grad_outer[None],
        grad_final[None],
    )


def solution(mesh):
    fine = Mesh(mesh.devices.reshape(8, 4, 2, 4), ("z", "y", "c", "mp"))
    both = (*DP, "mp")
    placed = (
        P(both, None),
        P(both, None),
        P(),
        P(None, None, DP, "mp"),
        P(None, "mp", DP),
        P(None, DP, "mp"),
        P(None, "mp", DP),
        P(DP, None),
        P(DP, None),
        P(DP, None, None),
        P(DP, None, None),
        P(),
        P(DP, None, None),
        P(DP, None, None),
        P(DP, None, None),
        P(DP, None, None),
        P(DP, None, None),
        P(DP, None, None),
    )
    return jax.shard_map(
        on_device,
        mesh=fine,
        in_specs=placed,
        out_specs=(
            P(both, None, None),
            P(DP, "mp", None),
            P(DP, None, None),
            P(DP, None, None),
            P(DP, None, None),
            P(DP, None, None),
            P(DP, None, None),
        ),
        check_vma=False,
    )
```

```python
import math

import jax
import jax.numpy as jnp
from jax import lax
from jax.experimental import pallas as pl
from jax.experimental.pallas import tpu as pltpu
from jax.sharding import Mesh, PartitionSpec as P

D = 768
HDIM = 64
EMB = 25
READ = 2
LEVELS = 20
ADIM_MAX = 14
ACT = 56
SEQ = 64
F32 = jnp.float32
BF16 = jnp.bfloat16
DP = ("z", "y", "c")


norm_eps = 1e-05


def sent_to_all(x, axis):
    copies = jnp.broadcast_to(x, (lax.axis_size(axis), *x.shape))
    return lax.all_to_all(copies, axis, split_axis=0, concat_axis=0, tiled=True)


def summed_on_arrival(x, axis):
    pieces = x.reshape(lax.axis_size(axis), -1, x.shape[1])
    arrived = lax.all_to_all(pieces, axis, split_axis=0, concat_axis=0, tiled=True)
    return arrived.astype(F32).sum(axis=0)


def normalize(values, scale_gain):
    center = values - jnp.mean(values, axis=-1, keepdims=True)
    spread = jnp.mean(center * center, axis=-1, keepdims=True)
    return center * lax.rsqrt(spread + norm_eps) * scale_gain


def mm(a, b):
    return jnp.dot(a, b, preferred_element_type=F32)


def mm_t(a, b):
    return jnp.einsum("tk,dk->td", a, b, preferred_element_type=F32)


def allowed_keys(observed):
    length = observed.shape[1]
    position = jnp.arange(length)
    visible = (observed == 1) & (position < length - READ)[None, :]
    itself = position[:, None] == position[None, :]
    return visible[:, None, :] | itself[None, :, :]


def attend(queries, key_rows, value_rows, allowed):
    scores = jnp.einsum(
        "sqhd,skhd->shqk", queries, key_rows, preferred_element_type=F32
    ) * HDIM ** (-0.5)
    weights = jnp.where(allowed[:, None, :, :], jnp.exp(scores), 0.0)
    shares = (weights / jnp.sum(weights, axis=-1, keepdims=True)).astype(BF16)
    context = jnp.einsum("shqk,skhd->sqhd", shares, value_rows, preferred_element_type=F32)
    return context.astype(BF16)


def nt(a, b):
    return lax.dot_general(a, b, (((1,), (1,)), ((), ())), preferred_element_type=F32)


def trunk_rows_kernel(res_ref, mask_ref, gain_ref, all_ref, out_ref, mlp, att, mlp_sem, att_sem):
    def block(side, part):
        return pltpu.make_async_copy(
            all_ref.at[pl.ds(side * D, D), pl.ds(1536 * (part + 1), 1536)],
            mlp.at[side, part],
            mlp_sem.at[side, part],
        )

    def attention(side):
        return pltpu.make_async_copy(
            all_ref.at[pl.ds(side * D, D), pl.ds(0, 1536)], att.at[side], att_sem.at[side]
        )

    for side in range(2):
        for part in range(2):
            block(side, part).start()
    for side in range(2):
        attention(side).start()
    residual = res_ref[...]
    normed = normalize(residual, gain_ref[1:2, :]).astype(BF16)
    for side in range(2):
        block(side, 0).wait()
        hidden = jax.nn.gelu(mm(normed, mlp[side, 0]), approximate=True).astype(BF16)
        block(side, 1).wait()
        residual = residual + nt(hidden, mlp[side, 1])
    normed = normalize(residual, gain_ref[2:3, :])
    ends = [residual[SEQ * k + SEQ - READ : SEQ * (k + 1)] for k in (0, 1, 2, 2)]
    ending = jnp.concatenate(ends, axis=0)
    ends = [normed[SEQ * k + SEQ - READ : SEQ * (k + 1)] for k in (0, 1, 2, 2)]
    normed_end = jnp.concatenate(ends, axis=0).astype(BF16)
    normed = normed.astype(BF16)
    rows, keys, width = 48, residual.shape[0], 384
    row = lax.broadcasted_iota(jnp.int32, (rows, keys), 0) % 8
    key = lax.broadcasted_iota(jnp.int32, (rows, keys), 1)
    place = key % SEQ
    seen = (mask_ref[...] == 1) & (place < SEQ - READ)
    allowed = (key // SEQ == jnp.minimum(row // READ, 2)) & (
        seen | (place == SEQ - READ + row % READ)
    )
    own_head = (
        lax.broadcasted_iota(jnp.int32, (rows, width), 0) // 8
        == lax.broadcasted_iota(jnp.int32, (rows, width), 1) // HDIM
    )
    for side in range(2):
        attention(side).wait()
        queries = mm(normed_end, att[side, :, 0:384]).astype(BF16).astype(F32)
        key_rows = mm(normed, att[side, :, 384:768]).astype(BF16)
        value_rows = mm(normed, att[side, :, 768:1152]).astype(BF16)
        spread = jnp.where(own_head, jnp.concatenate([queries] * 6, axis=0), 0.0).astype(BF16)
        scores = nt(spread, key_rows) * HDIM ** (-0.5)
        weights = jnp.where(allowed, jnp.exp(scores), 0.0)
        shares = (weights / jnp.sum(weights, axis=-1, keepdims=True)).astype(BF16)
        context = jnp.where(own_head, mm(shares, value_rows), 0.0)
        context = sum(context[8 * k : 8 * k + 8] for k in range(6)).astype(BF16)
        ending = ending + nt(context, att[side, :, 1152:1536])
    for member in range(4):
        out_ref[member] = ending.astype(BF16)


def trunk_rows(residual, mask_row, gains, weights):
    vmem = pl.BlockSpec(memory_space=pltpu.VMEM)
    rows = (residual, mask_row, gains)
    return pl.pallas_call(
        trunk_rows_kernel,
        out_shape=jax.ShapeDtypeStruct((4, 8, D), BF16),
        in_specs=[vmem, vmem, vmem, pl.BlockSpec(memory_space=pl.ANY)],
        out_specs=vmem,
        scratch_shapes=[
            pltpu.VMEM((2, 2, D, 1536), BF16),
            pltpu.VMEM((2, D, 1536), BF16),
            pltpu.SemaphoreType.DMA((2, 2)),
            pltpu.SemaphoreType.DMA((2,)),
        ],
        compiler_params=pltpu.CompilerParams(vmem_limit_bytes=40 * 1024 * 1024),
        name="trunk_rows",
    )(*(pltpu.with_memory_space_constraint(a, pltpu.VMEM) for a in rows), weights)


def readout_mlp_kernel(end_ref, gain_ref, first_ref, second_ref, out_ref):
    normed = normalize(end_ref[...].astype(F32), gain_ref[3:4, :]).astype(BF16)
    total = jnp.zeros(end_ref.shape, F32)
    for side_ref in (first_ref, second_ref):
        hidden = jax.nn.gelu(mm(normed, side_ref[:, 0:384]), approximate=True).astype(BF16)
        total = total + nt(hidden, side_ref[:, 384:768])
    for member in range(4):
        out_ref[member] = total.astype(BF16)


def readout_mlp(ending, gains, first_side, second_side):
    vmem = pl.BlockSpec(memory_space=pltpu.VMEM)
    operands = (ending, gains, first_side, second_side)
    return pl.pallas_call(
        readout_mlp_kernel,
        out_shape=jax.ShapeDtypeStruct((4, *ending.shape), BF16),
        in_specs=[vmem] * 4,
        out_specs=vmem,
        name="readout_mlp",
    )(*(pltpu.with_memory_space_constraint(a, pltpu.VMEM) for a in operands))


def plan():
    steps_up = (jnp.arange(LEVELS, dtype=F32) + 1.0) / LEVELS
    anchor = math.cos(0.008 / 1.008 * math.pi / 2) ** 2
    return jnp.cos((steps_up + 0.008) / 1.008 * (math.pi / 2)) ** 2 / anchor


def noisy_pair(level_ids, clean, noise_draw, table):
    picked = (level_ids[..., None] == jnp.arange(LEVELS)).astype(F32)
    kept = jnp.sum(picked * table, axis=-1)[..., None]
    mixed = jnp.sqrt(kept) * clean.astype(F32) + jnp.sqrt(1.0 - kept) * noise_draw.astype(F32)
    return mixed.astype(BF16)


def tail(first, target, weight_mask, inner_weight, outer_weight, final_weight):
    active = jax.nn.silu(first).astype(BF16)
    inner = jnp.dot(active, inner_weight, preferred_element_type=F32)
    second = jax.nn.silu(inner).astype(BF16)
    hidden = first + jnp.dot(second, outer_weight, preferred_element_type=F32)
    third = jax.nn.silu(hidden).astype(BF16)
    predicted = jnp.dot(third, final_weight, preferred_element_type=F32)
    differ = predicted - target
    return 0.5 * jnp.sum(weight_mask * differ * differ)


def head_grads(first, inner_weight, outer_weight, final_weight, target, weight_mask):

    def head_loss(first_in, inner_in, outer_in, final_in):
        return tail(first_in, target, weight_mask, inner_in, outer_in, final_in)

    loss_value, pullback = jax.vjp(head_loss, first, inner_weight, outer_weight, final_weight)
    return pullback(jnp.ones((), F32))


def on_device(
    tokens,
    obs_mask,
    norm_gains,
    attn_in,
    attn_out,
    mlp_in,
    mlp_out,
    embodiment,
    levels,
    actions,
    noise,
    action_dims,
    head_read,
    head_act,
    time_table,
    block_in,
    block_out,
    head_out,
):
    width = attn_in.shape[3]
    heads = width // HDIM
    peers = lax.axis_size(DP)
    my_model = lax.axis_index("mp")
    my_owner = lax.axis_index(DP)

    full = jnp.concatenate(
        [
            jnp.moveaxis(attn_in[1], 0, 1).reshape(12, -1),
            attn_out[1].T,
            mlp_in[0],
            mlp_out[0].T,
        ],
        axis=1,
    )
    groups = full.shape[1] // width
    pieces = [full] + [
        lax.ppermute(full, "mp", [(k, k ^ step) for k in range(4)]) for step in (1, 2, 3)
    ]
    ordered = []
    for member in range(4):
        apart = my_model ^ member
        piece = pieces[3]
        for step in range(3):
            piece = jnp.where(apart == step, pieces[step], piece)
        ordered.append(piece)
    full = jnp.stack(ordered).reshape(2, 2, 12, groups, width)
    full = full.transpose(0, 2, 3, 1, 4).reshape(2, 12, -1)
    share = jnp.stack([mlp_in[1], mlp_out[1].T], axis=1).reshape(12, 2, 2, -1)
    share = share.transpose(2, 0, 1, 3).reshape(2, 12, -1)
    halves = jnp.concatenate([full, share], axis=2)
    upper = lax.axis_index("c") == 1
    mine = jnp.where(upper, halves[1], halves[0])
    other = lax.ppermute(jnp.where(upper, halves[0], halves[1]), "c", [(0, 1), (1, 0)])
    piece = jnp.concatenate(
        [jnp.where(upper, other, mine), jnp.where(upper, mine, other)], axis=0
    )

    owners = embodiment[:, 0]
    place = (jnp.arange(peers)[:, None] == owners[None, :]).astype(BF16)
    row_owner = jnp.pad(owners.reshape(4, 3), ((0, 0), (0, 1)), constant_values=-1)
    row_owner = jnp.repeat(row_owner.reshape(-1), READ)
    target = jnp.arange(peers * READ)
    row_place = (target[:, None] // READ == row_owner[None, :]) & (
        target[:, None] % READ == jnp.arange(row_owner.size)[None, :] % READ
    )
    row_place = row_place.astype(BF16)
    noisy = noisy_pair(levels, actions, noise, plan())
    marks = (levels + 1).astype(BF16)[..., None]
    early = jnp.concatenate([noisy, noise, marks, jnp.zeros((*levels.shape, 15), BF16)], axis=-1)
    sent = jnp.einsum("es,srf->erf", place, early, preferred_element_type=F32).astype(BF16)
    residual = tokens.astype(F32)
    normed = normalize(residual, norm_gains[0]).astype(BF16)
    mask_row = jnp.pad(obs_mask.reshape(1, -1).astype(BF16), ((0, 15), (0, D - obs_mask.size)))
    rows = jnp.concatenate([normed, mask_row], axis=0)
    first_piece = jnp.concatenate(
        [jnp.moveaxis(attn_in[0], 0, 1).reshape(12, -1), attn_out[0].T], axis=1
    )
    piece, rows = lax.optimization_barrier((piece, rows))
    gathered_weights = lax.all_gather(piece, ("c", "z", "y"), axis=0, tiled=True)

    arrived = sent_to_all(rows, "mp")
    for axis, step in (("z", 1), ("z", 2), ("z", 4), ("y", 1), ("y", 2), ("c", 1)):
        if step == 2 and axis == "y":
            first_piece, arrived = lax.optimization_barrier((first_piece, arrived))
        swapped = [(k, k ^ step) for k in range(lax.axis_size(axis))]
        other = lax.ppermute(first_piece, axis, swapped)
        upper = (lax.axis_index(axis) // step) % 2 == 1
        low = jnp.where(upper, other, first_piece)
        high = jnp.where(upper, first_piece, other)
        first_piece = jnp.concatenate([low, high], axis=0)
    index = jnp.arange(D)
    owner = index // 12
    held = (owner % 2) * 32 + (owner // 2 % 4) * 8 + owner // 8
    order = (held * 12 + index % 12)[:, None] == index[None, :]
    first_weight = mm(order.astype(BF16), first_piece).astype(BF16)
    own_rows = normed.shape[0]
    gathered = arrived[:, :own_rows].reshape(-1, D)
    mask_group = arrived[:, own_rows, :own_rows].astype(jnp.int32).reshape(-1, SEQ)
    samples = mask_group.shape[0]
    projected = mm(gathered, first_weight[:, : 3 * width]).astype(BF16)
    projected = jnp.moveaxis(projected.reshape(-1, 3, width), 1, 0)
    projected = projected.reshape(3, samples, SEQ, heads, HDIM)
    context = attend(projected[0], projected[1], projected[2], allowed_keys(mask_group))
    partial_value = mm_t(context.reshape(-1, width), first_weight[:, 3 * width :])
    partial_value, sent = lax.optimization_barrier((partial_value.astype(BF16), sent))
    residual = residual + summed_on_arrival(partial_value, "mp")
    got = lax.all_to_all(sent, DP, split_axis=0, concat_axis=0, tiled=True)
    got = got.reshape(peers * READ, 128)

    residual, got, gathered_weights = lax.optimization_barrier((residual, got, gathered_weights))
    sides = [gathered_weights[D * k : D * (k + 1), 4608:5376] for k in range(2)]
    copies = trunk_rows(residual, obs_mask.reshape(1, -1), norm_gains, gathered_weights)
    ending = lax.all_to_all(copies, "mp", split_axis=0, concat_axis=0, tiled=True)
    ending = ending.reshape(-1, D)
    copies = readout_mlp(ending, norm_gains, *sides)
    terms = lax.all_to_all(copies, "mp", split_axis=0, concat_axis=0, tiled=True)
    ending = ending.astype(F32) + terms.astype(F32).sum(axis=0)
    readouts = normalize(ending, norm_gains[4]).astype(BF16)

    send = mm(row_place, readouts).astype(BF16).reshape(peers, READ, D)
    features = lax.all_to_all(send, DP, split_axis=0, concat_axis=0, tiled=True)
    features = features.reshape(peers * READ, D)
    head_noisy = got[:, :ACT]
    head_target = got[:, ACT : 2 * ACT].astype(F32)
    head_level = got[:, 2 * ACT].astype(jnp.int32) - 1
    onehot = (head_level[:, None] == jnp.arange(LEVELS)).astype(BF16)
    dims_here = jnp.sum(jnp.where(jnp.arange(EMB) == my_owner, action_dims, 0))
    column = jnp.arange(ACT) % ADIM_MAX
    weight_mask = (head_level >= 0).astype(F32)[:, None] * (column < dims_here).astype(F32)[None, :]
    others = mm(head_noisy, head_act[0]) + mm(onehot, time_table[0])
    first = mm(features, head_read[0]) + others
    grad_first, grad_inner, grad_outer, grad_final = head_grads(
        first,
        block_in[0].astype(F32),
        block_out[0].astype(F32),
        head_out[0].astype(F32),
        head_target,
        weight_mask,
    )
    grad_bf = grad_first.astype(BF16)
    backward = jnp.einsum("nc,dc->nd", grad_bf, head_read[0], preferred_element_type=F32)
    backward = backward.astype(BF16).reshape(peers, READ, D)
    backward, features = lax.optimization_barrier((backward, features))
    arrived = lax.all_to_all(backward, DP, split_axis=0, concat_axis=0, tiled=True)
    mine = samples // 4
    own_place = lax.dynamic_slice_in_dim(place, my_model * mine, mine, 1)
    arrived = jnp.einsum("es,erf->srf", own_place, arrived, preferred_element_type=F32)
    arrived = arrived.astype(BF16)
    part = lax.dynamic_slice_in_dim(features, my_model * width, width, 1)
    grad_read = jnp.einsum("nd,nc->dc", part, grad_bf, preferred_element_type=F32)
    grad_act = jnp.einsum("na,nc->ac", head_noisy, grad_bf, preferred_element_type=F32)
    grad_time = jnp.einsum("nl,nc->lc", onehot, grad_bf, preferred_element_type=F32)
    return (
        arrived,
        grad_read[None],
        grad_act[None],
        grad_time[None],
        grad_inner[None],
        grad_outer[None],
        grad_final[None],
    )


def solution(mesh):
    fine = Mesh(mesh.devices.reshape(8, 4, 2, 4), ("z", "y", "c", "mp"))
    both = (*DP, "mp")
    placed = (
        P(both, None),
        P(both, None),
        P(),
        P(None, None, DP, "mp"),
        P(None, "mp", DP),
        P(None, DP, "mp"),
        P(None, "mp", DP),
        P(DP, None),
        P(DP, None),
        P(DP, None, None),
        P(DP, None, None),
        P(),
        P(DP, None, None),
        P(DP, None, None),
        P(DP, None, None),
        P(DP, None, None),
        P(DP, None, None),
        P(DP, None, None),
    )
    return jax.shard_map(
        on_device,
        mesh=fine,
        in_specs=placed,
        out_specs=(
            P(both, None, None),
            P(DP, "mp", None),
            P(DP, None, None),
            P(DP, None, None),
            P(DP, None, None),
            P(DP, None, None),
            P(DP, None, None),
        ),
        check_vma=False,
    )
```

```python
import math

import jax
import jax.numpy as jnp
from jax import lax
from jax.experimental import pallas as pl
from jax.experimental.pallas import tpu as pltpu
from jax.sharding import Mesh, PartitionSpec as P

D = 768
HDIM = 64
EMB = 25
READ = 2
LEVELS = 20
ADIM_MAX = 14
ACT = 56
SEQ = 64
F32 = jnp.float32
BF16 = jnp.bfloat16
DP = ("z", "y", "c")


norm_eps = 1e-05


def sent_to_all(x, axis):
    copies = jnp.broadcast_to(x, (lax.axis_size(axis), *x.shape))
    return lax.all_to_all(copies, axis, split_axis=0, concat_axis=0, tiled=True)


def members_in_order(x):
    pieces = [x] + [lax.ppermute(x, "mp", [(k, k ^ step) for k in range(4)]) for step in (1, 2, 3)]
    ordered = []
    for member in range(4):
        apart = lax.axis_index("mp") ^ member
        piece = pieces[3]
        for step in range(3):
            piece = jnp.where(apart == step, pieces[step], piece)
        ordered.append(piece)
    return jnp.stack(ordered)


def summed_on_arrival(x, axis):
    pieces = x.reshape(lax.axis_size(axis), -1, x.shape[1])
    arrived = lax.all_to_all(pieces, axis, split_axis=0, concat_axis=0, tiled=True)
    return arrived.astype(F32).sum(axis=0)


def normalize(values, scale_gain):
    center = values - jnp.mean(values, axis=-1, keepdims=True)
    spread = jnp.mean(center * center, axis=-1, keepdims=True)
    return center * lax.rsqrt(spread + norm_eps) * scale_gain


def mm(a, b):
    return jnp.dot(a, b, preferred_element_type=F32)


def mm_t(a, b):
    return jnp.einsum("tk,dk->td", a, b, preferred_element_type=F32)


def allowed_keys(observed):
    length = observed.shape[1]
    position = jnp.arange(length)
    visible = (observed == 1) & (position < length - READ)[None, :]
    itself = position[:, None] == position[None, :]
    return visible[:, None, :] | itself[None, :, :]


def attend(queries, key_rows, value_rows, allowed):
    scores = jnp.einsum(
        "sqhd,skhd->shqk", queries, key_rows, preferred_element_type=F32
    ) * HDIM ** (-0.5)
    weights = jnp.where(allowed[:, None, :, :], jnp.exp(scores), 0.0)
    shares = (weights / jnp.sum(weights, axis=-1, keepdims=True)).astype(BF16)
    context = jnp.einsum("shqk,skhd->sqhd", shares, value_rows, preferred_element_type=F32)
    return context.astype(BF16)


def nt(a, b):
    return lax.dot_general(a, b, (((1,), (1,)), ((), ())), preferred_element_type=F32)


def trunk_rows_kernel(res_ref, mask_ref, gain_ref, all_ref, out_ref, mlp, att, mlp_sem, att_sem):
    def block(side, part):
        return pltpu.make_async_copy(
            all_ref.at[pl.ds(side * D, D), pl.ds(1536 * (part + 1), 1536)],
            mlp.at[side, part],
            mlp_sem.at[side, part],
        )

    def attention(side):
        return pltpu.make_async_copy(
            all_ref.at[pl.ds(side * D, D), pl.ds(0, 1536)], att.at[side], att_sem.at[side]
        )

    for side in range(2):
        for part in range(2):
            block(side, part).start()
    for side in range(2):
        attention(side).start()
    residual = res_ref[...]
    normed = normalize(residual, gain_ref[1:2, :]).astype(BF16)
    for side in range(2):
        block(side, 0).wait()
        hidden = jax.nn.gelu(mm(normed, mlp[side, 0]), approximate=True).astype(BF16)
        block(side, 1).wait()
        residual = residual + nt(hidden, mlp[side, 1])
    normed = normalize(residual, gain_ref[2:3, :])
    ends = [residual[SEQ * k + SEQ - READ : SEQ * (k + 1)] for k in (0, 1, 2, 2)]
    ending = jnp.concatenate(ends, axis=0)
    ends = [normed[SEQ * k + SEQ - READ : SEQ * (k + 1)] for k in (0, 1, 2, 2)]
    normed_end = jnp.concatenate(ends, axis=0).astype(BF16)
    normed = normed.astype(BF16)
    rows, keys, width = 48, residual.shape[0], 384
    row = lax.broadcasted_iota(jnp.int32, (rows, keys), 0) % 8
    key = lax.broadcasted_iota(jnp.int32, (rows, keys), 1)
    place = key % SEQ
    seen = (mask_ref[...] == 1) & (place < SEQ - READ)
    allowed = (key // SEQ == jnp.minimum(row // READ, 2)) & (
        seen | (place == SEQ - READ + row % READ)
    )
    own_head = (
        lax.broadcasted_iota(jnp.int32, (rows, width), 0) // 8
        == lax.broadcasted_iota(jnp.int32, (rows, width), 1) // HDIM
    )
    for side in range(2):
        attention(side).wait()
        queries = mm(normed_end, att[side, :, 0:384]).astype(BF16).astype(F32)
        key_rows = mm(normed, att[side, :, 384:768]).astype(BF16)
        value_rows = mm(normed, att[side, :, 768:1152]).astype(BF16)
        spread = jnp.where(own_head, jnp.concatenate([queries] * 6, axis=0), 0.0).astype(BF16)
        scores = nt(spread, key_rows) * HDIM ** (-0.5)
        weights = jnp.where(allowed, jnp.exp(scores), 0.0)
        shares = (weights / jnp.sum(weights, axis=-1, keepdims=True)).astype(BF16)
        context = jnp.where(own_head, mm(shares, value_rows), 0.0)
        context = sum(context[8 * k : 8 * k + 8] for k in range(6)).astype(BF16)
        ending = ending + nt(context, att[side, :, 1152:1536])
    out_ref[...] = ending.astype(BF16)


def trunk_rows(residual, mask_row, gains, weights):
    vmem = pl.BlockSpec(memory_space=pltpu.VMEM)
    rows = (residual, mask_row, gains)
    return pl.pallas_call(
        trunk_rows_kernel,
        out_shape=jax.ShapeDtypeStruct((8, D), BF16),
        in_specs=[vmem, vmem, vmem, pl.BlockSpec(memory_space=pl.ANY)],
        out_specs=vmem,
        scratch_shapes=[
            pltpu.VMEM((2, 2, D, 1536), BF16),
            pltpu.VMEM((2, D, 1536), BF16),
            pltpu.SemaphoreType.DMA((2, 2)),
            pltpu.SemaphoreType.DMA((2,)),
        ],
        compiler_params=pltpu.CompilerParams(vmem_limit_bytes=40 * 1024 * 1024),
        name="trunk_rows",
    )(*(pltpu.with_memory_space_constraint(a, pltpu.VMEM) for a in rows), weights)


def readout_mlp_kernel(end_ref, gain_ref, first_ref, second_ref, out_ref):
    normed = normalize(end_ref[...].astype(F32), gain_ref[3:4, :]).astype(BF16)
    total = jnp.zeros(end_ref.shape, F32)
    for side_ref in (first_ref, second_ref):
        hidden = jax.nn.gelu(mm(normed, side_ref[:, 0:384]), approximate=True).astype(BF16)
        total = total + nt(hidden, side_ref[:, 384:768])
    out_ref[...] = total.astype(BF16)


def readout_mlp(ending, gains, first_side, second_side):
    vmem = pl.BlockSpec(memory_space=pltpu.VMEM)
    operands = (ending, gains, first_side, second_side)
    return pl.pallas_call(
        readout_mlp_kernel,
        out_shape=jax.ShapeDtypeStruct(ending.shape, BF16),
        in_specs=[vmem] * 4,
        out_specs=vmem,
        name="readout_mlp",
    )(*(pltpu.with_memory_space_constraint(a, pltpu.VMEM) for a in operands))


def plan():
    steps_up = (jnp.arange(LEVELS, dtype=F32) + 1.0) / LEVELS
    anchor = math.cos(0.008 / 1.008 * math.pi / 2) ** 2
    return jnp.cos((steps_up + 0.008) / 1.008 * (math.pi / 2)) ** 2 / anchor


def noisy_pair(level_ids, clean, noise_draw, table):
    picked = (level_ids[..., None] == jnp.arange(LEVELS)).astype(F32)
    kept = jnp.sum(picked * table, axis=-1)[..., None]
    mixed = jnp.sqrt(kept) * clean.astype(F32) + jnp.sqrt(1.0 - kept) * noise_draw.astype(F32)
    return mixed.astype(BF16)


def tail(first, target, weight_mask, inner_weight, outer_weight, final_weight):
    active = jax.nn.silu(first).astype(BF16)
    inner = jnp.dot(active, inner_weight, preferred_element_type=F32)
    second = jax.nn.silu(inner).astype(BF16)
    hidden = first + jnp.dot(second, outer_weight, preferred_element_type=F32)
    third = jax.nn.silu(hidden).astype(BF16)
    predicted = jnp.dot(third, final_weight, preferred_element_type=F32)
    differ = predicted - target
    return 0.5 * jnp.sum(weight_mask * differ * differ)


def head_grads(first, inner_weight, outer_weight, final_weight, target, weight_mask):

    def head_loss(first_in, inner_in, outer_in, final_in):
        return tail(first_in, target, weight_mask, inner_in, outer_in, final_in)

    loss_value, pullback = jax.vjp(head_loss, first, inner_weight, outer_weight, final_weight)
    return pullback(jnp.ones((), F32))


def on_device(
    tokens,
    obs_mask,
    norm_gains,
    attn_in,
    attn_out,
    mlp_in,
    mlp_out,
    embodiment,
    levels,
    actions,
    noise,
    action_dims,
    head_read,
    head_act,
    time_table,
    block_in,
    block_out,
    head_out,
):
    width = attn_in.shape[3]
    heads = width // HDIM
    peers = lax.axis_size(DP)
    my_model = lax.axis_index("mp")
    my_owner = lax.axis_index(DP)

    full = jnp.concatenate(
        [
            jnp.moveaxis(attn_in[1], 0, 1).reshape(12, -1),
            attn_out[1].T,
            mlp_in[0],
            mlp_out[0].T,
        ],
        axis=1,
    )
    groups = full.shape[1] // width
    full = members_in_order(full).reshape(2, 2, 12, groups, width)
    full = full.transpose(0, 2, 3, 1, 4).reshape(2, 12, -1)
    share = jnp.stack([mlp_in[1], mlp_out[1].T], axis=1).reshape(12, 2, 2, -1)
    share = share.transpose(2, 0, 1, 3).reshape(2, 12, -1)
    halves = jnp.concatenate([full, share], axis=2)
    upper = lax.axis_index("c") == 1
    mine = jnp.where(upper, halves[1], halves[0])
    other = lax.ppermute(jnp.where(upper, halves[0], halves[1]), "c", [(0, 1), (1, 0)])
    piece = jnp.concatenate(
        [jnp.where(upper, other, mine), jnp.where(upper, mine, other)], axis=0
    )

    owners = embodiment[:, 0]
    place = (jnp.arange(peers)[:, None] == owners[None, :]).astype(BF16)
    row_owner = jnp.pad(owners.reshape(4, 3), ((0, 0), (0, 1)), constant_values=-1)
    row_owner = jnp.repeat(row_owner.reshape(-1), READ)
    target = jnp.arange(peers * READ)
    row_place = (target[:, None] // READ == row_owner[None, :]) & (
        target[:, None] % READ == jnp.arange(row_owner.size)[None, :] % READ
    )
    row_place = row_place.astype(BF16)
    noisy = noisy_pair(levels, actions, noise, plan())
    marks = (levels + 1).astype(BF16)[..., None]
    early = jnp.concatenate([noisy, noise, marks, jnp.zeros((*levels.shape, 15), BF16)], axis=-1)
    sent = jnp.einsum("es,srf->erf", place, early, preferred_element_type=F32).astype(BF16)
    residual = tokens.astype(F32)
    normed = normalize(residual, norm_gains[0]).astype(BF16)
    mask_row = jnp.pad(obs_mask.reshape(1, -1).astype(BF16), ((0, 15), (0, D - obs_mask.size)))
    rows = jnp.concatenate([normed, mask_row], axis=0)
    first_piece = jnp.concatenate(
        [jnp.moveaxis(attn_in[0], 0, 1).reshape(12, -1), attn_out[0].T], axis=1
    )
    piece, rows = lax.optimization_barrier((piece, rows))
    gathered_weights = lax.all_gather(piece, ("c", "z", "y"), axis=0, tiled=True)

    arrived = sent_to_all(rows, "mp")
    for axis, step in (("z", 1), ("z", 2), ("z", 4), ("y", 1), ("y", 2), ("c", 1)):
        if step == 2 and axis == "y":
            first_piece, arrived = lax.optimization_barrier((first_piece, arrived))
        swapped = [(k, k ^ step) for k in range(lax.axis_size(axis))]
        other = lax.ppermute(first_piece, axis, swapped)
        upper = (lax.axis_index(axis) // step) % 2 == 1
        low = jnp.where(upper, other, first_piece)
        high = jnp.where(upper, first_piece, other)
        first_piece = jnp.concatenate([low, high], axis=0)
    index = jnp.arange(D)
    owner = index // 12
    held = (owner % 2) * 32 + (owner // 2 % 4) * 8 + owner // 8
    order = (held * 12 + index % 12)[:, None] == index[None, :]
    first_weight = mm(order.astype(BF16), first_piece).astype(BF16)
    own_rows = normed.shape[0]
    gathered = arrived[:, :own_rows].reshape(-1, D)
    mask_group = arrived[:, own_rows, :own_rows].astype(jnp.int32).reshape(-1, SEQ)
    samples = mask_group.shape[0]
    projected = mm(gathered, first_weight[:, : 3 * width]).astype(BF16)
    projected = jnp.moveaxis(projected.reshape(-1, 3, width), 1, 0)
    projected = projected.reshape(3, samples, SEQ, heads, HDIM)
    context = attend(projected[0], projected[1], projected[2], allowed_keys(mask_group))
    partial_value = mm_t(context.reshape(-1, width), first_weight[:, 3 * width :])
    partial_value, sent = lax.optimization_barrier((partial_value.astype(BF16), sent))
    residual = residual + summed_on_arrival(partial_value, "mp")
    got = lax.all_to_all(sent, DP, split_axis=0, concat_axis=0, tiled=True)
    got = got.reshape(peers * READ, 128)

    residual, got, gathered_weights = lax.optimization_barrier((residual, got, gathered_weights))
    sides = [gathered_weights[D * k : D * (k + 1), 4608:5376] for k in range(2)]
    copies = trunk_rows(residual, obs_mask.reshape(1, -1), norm_gains, gathered_weights)
    ending = members_in_order(copies).reshape(-1, D)
    copies = readout_mlp(ending, norm_gains, *sides)
    terms = members_in_order(copies)
    ending = ending.astype(F32) + terms.astype(F32).sum(axis=0)
    readouts = normalize(ending, norm_gains[4]).astype(BF16)

    send = mm(row_place, readouts).astype(BF16).reshape(peers, READ, D)
    features = lax.all_to_all(send, DP, split_axis=0, concat_axis=0, tiled=True)
    features = features.reshape(peers * READ, D)
    head_noisy = got[:, :ACT]
    head_target = got[:, ACT : 2 * ACT].astype(F32)
    head_level = got[:, 2 * ACT].astype(jnp.int32) - 1
    onehot = (head_level[:, None] == jnp.arange(LEVELS)).astype(BF16)
    dims_here = jnp.sum(jnp.where(jnp.arange(EMB) == my_owner, action_dims, 0))
    column = jnp.arange(ACT) % ADIM_MAX
    weight_mask = (head_level >= 0).astype(F32)[:, None] * (column < dims_here).astype(F32)[None, :]
    others = mm(head_noisy, head_act[0]) + mm(onehot, time_table[0])
    first = mm(features, head_read[0]) + others
    grad_first, grad_inner, grad_outer, grad_final = head_grads(
        first,
        block_in[0].astype(F32),
        block_out[0].astype(F32),
        head_out[0].astype(F32),
        head_target,
        weight_mask,
    )
    grad_bf = grad_first.astype(BF16)
    backward = jnp.einsum("nc,dc->nd", grad_bf, head_read[0], preferred_element_type=F32)
    backward = backward.astype(BF16).reshape(peers, READ, D)
    backward, features = lax.optimization_barrier((backward, features))
    arrived = lax.all_to_all(backward, DP, split_axis=0, concat_axis=0, tiled=True)
    mine = samples // 4
    own_place = lax.dynamic_slice_in_dim(place, my_model * mine, mine, 1)
    arrived = jnp.einsum("es,erf->srf", own_place, arrived, preferred_element_type=F32)
    arrived = arrived.astype(BF16)
    part = lax.dynamic_slice_in_dim(features, my_model * width, width, 1)
    grad_read = jnp.einsum("nd,nc->dc", part, grad_bf, preferred_element_type=F32)
    grad_act = jnp.einsum("na,nc->ac", head_noisy, grad_bf, preferred_element_type=F32)
    grad_time = jnp.einsum("nl,nc->lc", onehot, grad_bf, preferred_element_type=F32)
    return (
        arrived,
        grad_read[None],
        grad_act[None],
        grad_time[None],
        grad_inner[None],
        grad_outer[None],
        grad_final[None],
    )


def solution(mesh):
    fine = Mesh(mesh.devices.reshape(8, 4, 2, 4), ("z", "y", "c", "mp"))
    both = (*DP, "mp")
    placed = (
        P(both, None),
        P(both, None),
        P(),
        P(None, None, DP, "mp"),
        P(None, "mp", DP),
        P(None, DP, "mp"),
        P(None, "mp", DP),
        P(DP, None),
        P(DP, None),
        P(DP, None, None),
        P(DP, None, None),
        P(),
        P(DP, None, None),
        P(DP, None, None),
        P(DP, None, None),
        P(DP, None, None),
        P(DP, None, None),
        P(DP, None, None),
    )
    return jax.shard_map(
        on_device,
        mesh=fine,
        in_specs=placed,
        out_specs=(
            P(both, None, None),
            P(DP, "mp", None),
            P(DP, None, None),
            P(DP, None, None),
            P(DP, None, None),
            P(DP, None, None),
            P(DP, None, None),
        ),
        check_vma=False,
    )
```
